32 devices in a mesh: dp: 8 (over y, x, core), tensor: 4 (over z).
Axes of the slice: x: 2, y: 2, z: 4, core: 2. Of those that a mesh axis runs over, the one named last changes fastest.
Arguments:
- tokens: bfloat16 [16384, 2048], P(('dp', 'tensor')), may hold values from -6 to 6
- segment_ids: int32 [8, 2048], P('dp'), may hold values from 0 to 15, never falling along the last dimension, each value on 1 to 1024 neighbouring positions
- attngain: float32 [2048], replicated, may hold values from 0.5 to 1.5
- attnshift: float32 [2048], replicated, may hold values from -1.75 to 1.75
- queryweight: bfloat16 [2048, 2048], P('dp', 'tensor'), may hold values from -0.125 to 0.125
- querybias: float32 [2048], P('tensor'), may hold values from -3 to 3
- keyvalue: bfloat16 [2048, 256], P('dp'), may hold values from -0.125 to 0.125
- valuebias: float32 [128], replicated, may hold values from -0.3125 to 0.3125
- outweight: bfloat16 [2048, 2048], P('tensor', 'dp'), may hold values from -0.75 to 0.75
- outbias: float32 [2048], replicated, may hold values from -3 to 3
- mlpgain: float32 [2048], replicated, may hold values from 0.5 to 1.5
- mlpshift: float32 [2048], replicated, may hold values from -1.75 to 1.75
- upweight: bfloat16 [2048, 8192], P('dp', 'tensor'), may hold values from -0.125 to 0.125
- upbias: float32 [8192], P('tensor'), may hold values from -3 to 3
- downweight: bfloat16 [8192, 2048], P('tensor', 'dp'), may hold values from -0.0625 to 0.0625
- downbias: float32 [2048], replicated, may hold values from -3 to 3
- cotangent: bfloat16 [16384, 2048], P(('dp', 'tensor')), may hold values from -6 to 6
Outputs:
- layer_output: bfloat16 [16384, 2048], P(('dp', 'tensor'))
- tokens_grad: bfloat16 [16384, 2048], P(('dp', 'tensor'))
- attngain_grad: float32 [2048], replicated
- attnshift_grad: float32 [2048], replicated
- queryweight_grad: float32 [2048, 2048], P('dp', 'tensor')
- querybias_grad: float32 [2048], P('tensor')
- keyvalue_grad: float32 [2048, 256], P('dp')
- valuebias_grad: float32 [128], replicated
- outweight_grad: float32 [2048, 2048], P('tensor', 'dp')
- outbias_grad: float32 [2048], replicated
- mlpgain_grad: float32 [2048], replicated
- mlpshift_grad: float32 [2048], replicated
- upweight_grad: float32 [2048, 8192], P('dp', 'tensor')
- upbias_grad: float32 [8192], P('tensor')
- downweight_grad: float32 [8192, 2048], P('tensor', 'dp')
- downbias_grad: float32 [2048], replicated
The draws below stay inside these ranges and needn't reach their ends.
Inputs may be any that keep to these rules, and one draw needn't show every extreme that they name: `segment_ids`: along each sequence the document numbers never fall.
All inputs are finite; a program needn't handle non-finite values.
Results may differ from the reference program's by a relative error of at most 0.015.
Values may be sent and summed in bfloat16 or wider, within the bound.
No kernel may reach another device: no remote copies, remote signals or barrier semaphores. Data moves between devices by JAX's collectives and lax.ppermute only.
A program may use at most 256 MiB of HBM per device.

```python
import math
import jax
import jax.numpy as jnp
import numpy as np
from jax import lax

D = 2048
HEADS = 16
HEAD_DIM = 128
FF = 8192
SEQ_LEN = 2048
DOCS = 16
TOKENS = 16384
N_DP = 8


def spiked(values, stream_key, source, target, parts, factor):
    owner, partner = [(jnp.arange(values.shape[axis_at]) // (values.shape[axis_at] // parts)).reshape([-1 if axis == axis_at else 1 for axis in range(values.ndim)]) for axis_at in (source, target)]
    chosen = jax.random.permutation(stream_key, parts)[partner]
    strong = (owner == chosen) | (owner == (partner + parts // 2) % parts)
    return jnp.where(strong, factor * values, values)


def block_scale(stream_key, dims, shards, low, high):
    def one(axis_at, parts):
        steps = jax.random.uniform(jax.random.fold_in(jax.random.fold_in(stream_key, 6), axis_at), (parts,), jnp.float32, low / len(shards), high / len(shards))
        return jnp.repeat(jnp.exp(steps), dims[axis_at] // parts).reshape((-1,) + (1,) * (len(dims) - axis_at - 1))

    factor_of = one(*shards[0])
    for cut in shards[1:]:
        factor_of = factor_of * one(*cut)
    return factor_of


def length_profile(count, total, bound, slope):
    portions = [(1 << 20) // math.isqrt(grade ** slope) + 1 for grade in range(2, count + 1)]
    rest, holding = total - bound - (count - 1), [1] * (count - 1)
    while rest > 0:
        candidates = [i for i in range(count - 1) if holding[i] < bound]
        pool, left = sum([portions[i] for i in candidates]), rest
        for i in candidates:
            more = min(bound - holding[i], max(1, left * portions[i] // pool), rest)
            holding[i] = holding[i] + more
            rest = rest - more
    return np.array([bound] + holding)


def ragged_sizes(key, amount, total, limit, slope):
    if amount == 2:
        one = jax.random.randint(key, (), max(1, total - limit), min(limit, total - 1) + 1)
        return jnp.stack([one, total - one])
    tallies = jnp.asarray(length_profile(amount, total, limit, slope), jnp.int32)
    pairs = (amount - 1) // 2
    giver, receiver = tallies[1:1 + 2 * pairs:2], tallies[2:2 + 2 * pairs:2]
    room = jnp.minimum(giver - 1, limit - receiver)
    passed = jax.random.randint(jax.random.fold_in(key, 1), (pairs,), 0, 1 << 20) % (room + 1)
    tallies = tallies.at[1:1 + 2 * pairs:2].set(giver - passed).at[2:2 + 2 * pairs:2].set(receiver + passed)
    return tallies[jax.random.permutation(jax.random.fold_in(key, 2), amount)]


def gaussian(key, extent, deviation, most, shards=(), kind=jnp.bfloat16):
    loudness = block_scale(key, extent, shards, -0.22, 0.18) if shards else 1.0
    values = jax.random.normal(key, extent, jnp.float32) * deviation * loudness
    return jnp.minimum(jnp.maximum(values, -most), most).astype(kind)


def bell_draw_with(own_key, shape, scale, most, split, heavy, kind=jnp.bfloat16):
    result = scale * jax.random.normal(own_key, shape, jnp.float32)
    if split:
        result = result * block_scale(own_key, shape, split, -0.22, 0.18)
    return jnp.clip(spiked(result, jax.random.fold_in(own_key, 3), *heavy), -most, most).astype(kind)


def setup_inputs(seed: int = 0) -> dict:
    keys = jax.random.split(jax.random.key(seed), 18)
    return {
        "tokens": gaussian(keys[0], (TOKENS, D), 1.0, 6.0, ((0, 32),)),
        "segment_ids": jax.vmap(lambda own: jnp.searchsorted(jnp.cumsum(ragged_sizes(own, DOCS, SEQ_LEN, SEQ_LEN // 2, 2)), jnp.arange(SEQ_LEN), side="right"))(jax.random.split(keys[1], N_DP)).reshape((N_DP, SEQ_LEN)).astype(jnp.int32),
        "attngain": jnp.clip(1.0 + 0.1 * jax.random.normal(keys[2], (D,), jnp.float32), 0.5, 1.5),
        "attnshift": gaussian(keys[3], (D,), 0.3, 1.75, (), jnp.float32),
        "queryweight": gaussian(keys[4], (D, HEADS * HEAD_DIM), D ** -0.5, 0.125, ((0, 8), (1, 4))),
        "querybias": gaussian(keys[5], (HEADS * HEAD_DIM,), 0.5, 3.0, ((0, 4),), jnp.float32),
        "keyvalue": gaussian(keys[6], (D, 2 * HEAD_DIM), D ** -0.5, 0.125, ((0, 8),)),
        "valuebias": gaussian(keys[7], (HEAD_DIM,), 0.05, 0.3125, (), jnp.float32),
        "outweight": gaussian(keys[8], (HEADS * HEAD_DIM, D), (D // 32) ** -0.5, 0.75, ((0, 4), (1, 8))),
        "outbias": gaussian(keys[9], (D,), 0.5, 3.0, (), jnp.float32),
        "mlpgain": jnp.clip(1.0 + 0.1 * jax.random.normal(keys[10], (D,), jnp.float32), 0.5, 1.5),
        "mlpshift": gaussian(keys[11], (D,), 0.3, 1.75, (), jnp.float32),
        "upweight": gaussian(keys[12], (D, FF), D ** -0.5, 0.125, ((0, 8), (1, 4))),
        "upbias": gaussian(keys[13], (FF,), 0.5, 3.0, ((0, 4),), jnp.float32),
        "downweight": gaussian(keys[14], (FF, D), FF ** -0.5, 0.0625, ((0, 4), (1, 8))),
        "downbias": gaussian(keys[15], (D,), 0.5, 3.0, (), jnp.float32),
        "cotangent": bell_draw_with(keys[16], (TOKENS, D), 1.0, 6.0, ((0, 32),), (0, 1, 32, 2.75)),
    }


@jax.custom_vjp
def low(v):
    return lax.optimization_barrier(v.astype(jnp.bfloat16)).astype(jnp.float32)

@jax.custom_vjp
def low_back(v):
    return v

def low_keep(v):
    return (low(v), None)

def low_pass(kept, grad):
    return (grad,)

def back_keep(v):
    return (v, None)

def back_low(kept, grad):
    return (low(grad),)
low.defvjp(low_keep, low_pass)
low_back.defvjp(back_keep, back_low)
eps_norm = 1e-05
highest = lax.Precision.HIGHEST

def twin_round(values):
    return low_back(low(values))

def layer_norm(values, norm_gain, norm_shift):
    row_mean = lax.optimization_barrier(jnp.mean(values, axis=-1, keepdims=True))
    centered = values - row_mean
    row_var = lax.optimization_barrier(jnp.mean(centered * centered, axis=-1, keepdims=True))
    return centered * lax.rsqrt(row_var + eps_norm) * norm_gain + norm_shift

def product(left_side, right_side):
    return jnp.dot(left_side, right_side, precision=highest, preferred_element_type=jnp.float32)

def attend(queries, key_rows, values, segment):
    length = key_rows.shape[0]
    block_rows = min(512, length)
    blocks = length // block_rows
    score_scale = HEAD_DIM ** (-0.5)
    places = jnp.arange(length, dtype=jnp.int32)

    def one_block(block_item):
        query_rows, first_row = block_item
        query_rows = query_rows.reshape(block_rows, HEADS, HEAD_DIM)
        scores = low_back(jnp.einsum('bhd,kd->bhk', query_rows, key_rows, precision=highest)) * score_scale
        positions = first_row + jnp.arange(block_rows, dtype=jnp.int32)
        query_seg = lax.dynamic_slice_in_dim(segment, first_row, block_rows)
        allowed = (query_seg[:, None] == segment[None, :]) & (places[None, :] <= positions[:, None])
        scores = jnp.where(allowed[:, None, :], scores, -1e+30)
        totals = jax.nn.logsumexp(scores, axis=-1, keepdims=True)
        weights = low(jnp.exp(scores - totals))
        mixed_rows = jnp.einsum('bhk,kd->bhd', weights, values, precision=highest)
        return mixed_rows.reshape(block_rows, HEADS * HEAD_DIM)
    starts = jnp.arange(blocks, dtype=jnp.int32) * block_rows
    mixed_rows = lax.map(jax.checkpoint(one_block), (queries.reshape(blocks, block_rows, HEADS * HEAD_DIM), starts))
    return mixed_rows.reshape(length, HEADS * HEAD_DIM)

def layer_one(params, seq_rows, segment):
    attngain, attnshift, queryweight, querybias, keyvalue, valuebias, outweight, outbias, mlpgain, mlpshift, upweight, upbias, downweight, downbias = params
    normed_first = low(layer_norm(seq_rows, attngain, attnshift))
    queries = twin_round(product(normed_first, queryweight) + querybias)
    key_rows = twin_round(product(normed_first, keyvalue[:, :HEAD_DIM]))
    values = twin_round(product(normed_first, keyvalue[:, HEAD_DIM:]) + valuebias)
    mixed_rows = twin_round(attend(queries, key_rows, values, segment))
    residual = seq_rows + low_back(product(mixed_rows, outweight) + outbias)
    normed_second = low(layer_norm(residual, mlpgain, mlpshift))
    preact = low_back(product(normed_second, upweight) + upbias)
    active = low(jax.nn.gelu(preact, approximate=True))
    return residual + low_back(product(active, downweight) + downbias)

def reference(tokens, segment_ids, attngain, attnshift, queryweight, querybias, keyvalue, valuebias, outweight, outbias, mlpgain, mlpshift, upweight, upbias, downweight, downbias, cotangent):
    params = tuple((member.astype(jnp.float32) for member in (attngain, attnshift, queryweight, querybias, keyvalue, valuebias, outweight, outbias, mlpgain, mlpshift, upweight, upbias, downweight, downbias)))
    seq_rows = tokens.astype(jnp.float32).reshape(N_DP, SEQ_LEN, D)

    def forward(all_rows, weights_all):

        def scan_step(carried, pieces):
            return (carried, layer_one(weights_all, pieces[0], pieces[1]))
        _, outputs_all = lax.scan(scan_step, jnp.zeros((), jnp.float32), (all_rows, segment_ids))
        return outputs_all
    outputs_all, pullback = jax.vjp(forward, seq_rows, params)
    grad_rows, grad_params = pullback(cotangent.astype(jnp.float32).reshape(N_DP, SEQ_LEN, D))
    return (outputs_all.reshape(TOKENS, D).astype(jnp.bfloat16), grad_rows.reshape(TOKENS, D).astype(jnp.bfloat16), grad_params[0], grad_params[1], grad_params[2], grad_params[3], grad_params[4], grad_params[5], grad_params[6], grad_params[7], grad_params[8], grad_params[9], grad_params[10], grad_params[11], grad_params[12], grad_params[13])
```

```python
import functools

import jax
import jax.numpy as jnp
from jax import lax
from jax.experimental import pallas as pl
from jax.experimental.pallas import tpu as pltpu
from jax.sharding import PartitionSpec as P

eps_norm = 1e-05
masked_score = -1e30
bf16 = jnp.bfloat16
f32 = jnp.float32


def dot_nn(left_side, right_side):
    return jnp.dot(left_side, right_side, preferred_element_type=f32)


def dot_tn(left_side, right_side):
    return lax.dot_general(
        left_side, right_side, (((0,), (0,)), ((), ())), preferred_element_type=f32
    )


def dot_nt(left_side, right_side):
    return lax.dot_general(
        left_side, right_side, (((1,), (1,)), ((), ())), preferred_element_type=f32
    )


def norm_stats(values):
    row_mean = jnp.mean(values, axis=-1, keepdims=True)
    centered = values - row_mean
    row_var = jnp.mean(centered * centered, axis=-1, keepdims=True)
    scale = lax.rsqrt(row_var + eps_norm)
    return row_mean, scale


def norm_backward(values, row_mean, scale, gain, grad):
    xhat = (values - row_mean) * scale
    u = grad * gain
    u_mean = jnp.mean(u, axis=-1, keepdims=True)
    ux_mean = jnp.mean(u * xhat, axis=-1, keepdims=True)
    grad_in = (u - u_mean - xhat * ux_mean) * scale
    return grad_in, jnp.sum(grad * xhat, axis=0), jnp.sum(grad, axis=0)


gelu_c = 0.7978845608028654


def gelu_both(v):
    square = v * v
    inner = gelu_c * v * (1.0 + 0.044715 * square)
    t = jnp.tanh(inner)
    half = 0.5 * (1.0 + t)
    value = v * half
    slope = half + 0.5 * v * (1.0 - t * t) * (gelu_c * (1.0 + 3.0 * 0.044715 * square))
    return value, slope


def stack_heads(block, heads, width):
    return jnp.concatenate(
        [block[:, h * width : (h + 1) * width] for h in range(heads)], axis=0
    )


def block_bias(first_key, keys, start_row, query_row):
    key_at = first_key + lax.broadcasted_iota(jnp.int32, (keys, start_row.shape[1]), 0)
    allowed = (key_at >= start_row) & (key_at <= query_row)
    return jnp.where(allowed, 0.0, masked_score)


def attend_forward_kernel(
    heads, width, keys, info_ref, q_ref, kv_ref, start_ref, o_ref, total_ref
):
    at = pl.program_id(1)
    rows = q_ref.shape[0]
    q = stack_heads(q_ref[...], heads, width)
    start_row = start_ref[...]
    query_row = info_ref[2, at] + lax.broadcasted_iota(jnp.int32, (1, rows), 1)
    scale = width**-0.5

    def step(block, carried):
        top, total, mixed = carried
        first_key = pl.multiple_of(block * keys, keys)
        k = kv_ref[pl.ds(first_key, keys), :width]
        v = kv_ref[pl.ds(first_key, keys), width:]
        bias = block_bias(first_key, keys, start_row, query_row)
        scores = dot_nt(k, q) * scale + jnp.concatenate([bias] * heads, axis=1)
        new_top = jnp.maximum(top, jnp.max(scores, axis=0, keepdims=True))
        shrink = jnp.exp(top - new_top)
        part = jnp.exp(scores - new_top)
        total = total * shrink + jnp.sum(part, axis=0, keepdims=True)
        mixed = mixed * shrink + dot_tn(v, part.astype(bf16))
        return new_top, total, mixed

    count = heads * rows
    top, total, mixed = lax.fori_loop(
        info_ref[0, at],
        info_ref[1, at],
        step,
        (
            jnp.full((1, count), masked_score, f32),
            jnp.zeros((1, count), f32),
            jnp.zeros((width, count), f32),
        ),
    )
    out = (mixed / total).T.astype(bf16)
    for h in range(heads):
        o_ref[:, h * width : (h + 1) * width] = out[h * rows : (h + 1) * rows]
    total_ref[...] = (top + jnp.log(total)).reshape(total_ref.shape)


def attend_backward_kernel(
    heads,
    width,
    keys,
    info_ref,
    q_ref,
    grad_ref,
    o_ref,
    kv_ref,
    start_ref,
    total_ref,
    dq_ref,
    dkv_ref,
):
    at = pl.program_id(1)
    rows = q_ref.shape[0]

    @pl.when((pl.program_id(0) == 0) & (at == 0))
    def _():
        dkv_ref[...] = jnp.zeros_like(dkv_ref)

    q = stack_heads(q_ref[...], heads, width)
    grad = stack_heads(grad_ref[...], heads, width)
    out = stack_heads(o_ref[...], heads, width)
    delta = jnp.sum((grad.astype(f32) * out.astype(f32)).T, axis=0, keepdims=True)
    count = heads * rows
    total = total_ref[...].reshape(1, count)
    start_row = start_ref[...]
    query_row = info_ref[2, at] + lax.broadcasted_iota(jnp.int32, (1, rows), 1)
    scale = width**-0.5

    def step(block, dq):
        first_key = pl.multiple_of(block * keys, keys)
        k = kv_ref[pl.ds(first_key, keys), :width]
        v = kv_ref[pl.ds(first_key, keys), width:]
        bias = block_bias(first_key, keys, start_row, query_row)
        scores = dot_nt(k, q) * scale + jnp.concatenate([bias] * heads, axis=1)
        probs = jnp.exp(scores - total)
        dprobs = dot_nt(v, grad)
        dscores = (probs * (dprobs - delta) * scale).astype(bf16)
        dkv_ref[pl.ds(first_key, keys), :width] += dot_nn(dscores, q)
        dkv_ref[pl.ds(first_key, keys), width:] += dot_nn(probs.astype(bf16), grad)
        return dq + dot_tn(k, dscores)

    dq = lax.fori_loop(
        info_ref[0, at], info_ref[1, at], step, jnp.zeros((width, count), f32)
    )
    dq = dq.T.astype(bf16)
    for h in range(heads):
        dq_ref[:, h * width : (h + 1) * width] = dq[h * rows : (h + 1) * rows]


def attend_shapes(qkv, width):
    tokens = qkv.shape[0]
    heads_all = qkv.shape[1] // width - 2
    heads = 4 if heads_all % 4 == 0 else 1
    rows = min(128, tokens)
    return tokens, heads_all, heads, heads_all // heads, rows, tokens // rows


def attend_forward(qkv, kv_all, info, starts, width, keys):
    tokens, heads_all, heads, groups, rows, blocks = attend_shapes(qkv, width)
    return pl.pallas_call(
        functools.partial(attend_forward_kernel, heads, width, keys),
        grid_spec=pltpu.PrefetchScalarGridSpec(
            num_scalar_prefetch=1,
            grid=(groups, blocks),
            in_specs=[
                pl.BlockSpec((rows, heads * width), lambda g, i, info: (i, g)),
                pl.BlockSpec(kv_all.shape, lambda g, i, info: (0, 0)),
                pl.BlockSpec((1, rows), lambda g, i, info: (0, i)),
            ],
            out_specs=[
                pl.BlockSpec((rows, heads * width), lambda g, i, info: (i, g)),
                pl.BlockSpec((1, 1, 1, heads * rows), lambda g, i, info: (g, i, 0, 0)),
            ],
        ),
        out_shape=[
            jax.ShapeDtypeStruct((tokens, heads_all * width), bf16),
            jax.ShapeDtypeStruct((groups, blocks, 1, heads * rows), f32),
        ],
        name="attend_forward",
    )(info, qkv, kv_all, starts)


def attend_backward(qkv, grad, mixed, kv_all, info, starts, totals, width, keys):
    tokens, heads_all, heads, groups, rows, blocks = attend_shapes(qkv, width)
    tile = pl.BlockSpec((rows, heads * width), lambda g, i, info: (i, g))
    return pl.pallas_call(
        functools.partial(attend_backward_kernel, heads, width, keys),
        grid_spec=pltpu.PrefetchScalarGridSpec(
            num_scalar_prefetch=1,
            grid=(groups, blocks),
            in_specs=[
                tile,
                tile,
                tile,
                pl.BlockSpec(kv_all.shape, lambda g, i, info: (0, 0)),
                pl.BlockSpec((1, rows), lambda g, i, info: (0, i)),
                pl.BlockSpec((1, 1, 1, heads * rows), lambda g, i, info: (g, i, 0, 0)),
            ],
            out_specs=[
                tile,
                pl.BlockSpec(kv_all.shape, lambda g, i, info: (0, 0)),
            ],
        ),
        out_shape=[
            jax.ShapeDtypeStruct((tokens, heads_all * width), bf16),
            jax.ShapeDtypeStruct(kv_all.shape, f32),
        ],
        name="attend_backward",
    )(info, qkv, grad, mixed, kv_all, starts, totals)


class Ring:
    def __init__(self, size):
        self.size = size
        self.chips = size // 2
        half = self.chips // 2
        if half:
            self.order = list(range(half)) + list(range(self.chips - 1, half - 1, -1))
        else:
            self.order = [0]
        n = self.chips
        self.right = [
            (2 * self.order[i] + k, 2 * self.order[(i + 1) % n] + k)
            for i in range(n)
            for k in (0, 1)
        ]
        self.left = [(b, a) for a, b in self.right]
        self.swap = [(i, i ^ 1) for i in range(size)]
        self.far = n // 2
        offsets = [0]
        for s in range(1, self.far):
            offsets += [s, -s]
        if self.far:
            offsets.append(self.far)
        self.offsets = offsets

    def owner(self, index, offset, other):
        place = [0] * self.chips
        for i, chip in enumerate(self.order):
            place[chip] = i
        chip = index // 2
        core = index % 2
        at = jnp.array(place, jnp.int32)[chip]
        there = jnp.array(self.order, jnp.int32)[(at + offset) % self.chips]
        return 2 * there + (1 - core if other else core)

    def send(self, value, pairs):
        return lax.ppermute(value, "dp", pairs)

    def gather(self, own):
        rows = own.shape[0]
        cut = rows // 2
        found = {0: own}
        from_left = from_right = own
        for s in range(1, self.far):
            from_left = self.send(from_left, self.right)
            from_right = self.send(from_right, self.left)
            found[-s] = from_left
            found[s] = from_right
        if self.far:
            low = self.send(from_left[:cut], self.right)
            high = self.send(from_right[cut:], self.left)
            found[self.far] = jnp.concatenate([low, high], axis=0)
        blocks = {}
        for offset in self.offsets:
            blocks[(offset, 0)] = found[offset]
            blocks[(offset, 1)] = self.send(found[offset], self.swap)
        return blocks

    def scatter_sum(self, part):
        summed = {}
        for offset in reversed(self.offsets):
            there = self.send(part(offset, 1).astype(bf16), self.swap)
            summed[offset] = part(offset, 0) + there.astype(f32)
        if not self.far:
            return summed[0]
        cut = summed[0].shape[0] // 2
        result = summed[0]
        for sign, pairs in ((1, self.right), (-1, self.left)):
            held = None
            for s in range(self.far, 0, -1):
                if s == self.far:
                    message = summed[s][:cut] if sign > 0 else summed[s][cut:]
                elif s == self.far - 1:
                    message = self.add_half(summed[sign * s], held, sign, cut)
                else:
                    message = summed[sign * s] + held
                held = self.send(message.astype(bf16), pairs).astype(f32)
            if self.far == 1:
                result = self.add_half(result, held, sign, cut)
            else:
                result = result + held
        return result

    def add_half(self, value, held, sign, cut):
        if sign > 0:
            return jnp.concatenate([value[:cut] + held, value[cut:]], axis=0)
        return jnp.concatenate([value[:cut], value[cut:] + held], axis=0)


def on_device(
    tokens,
    segment_ids,
    attngain,
    attnshift,
    queryweight,
    querybias,
    keyvalue,
    valuebias,
    outweight,
    outbias,
    mlpgain,
    mlpshift,
    upweight,
    upbias,
    downweight,
    downbias,
    cotangent,
):
    head_dim = valuebias.shape[0]
    count, model = tokens.shape
    n_dp = lax.axis_size("dp")
    n_tensor = lax.axis_size("tensor")
    dp_index = lax.axis_index("dp")
    tensor_index = lax.axis_index("tensor")
    ring = Ring(n_dp)
    order = [(o, c) for o in ring.offsets for c in (0, 1)]
    segment = segment_ids[0]
    length = segment.shape[0]
    rows = tokens.astype(f32)
    depth = queryweight.shape[0]
    width = queryweight.shape[1]

    out_turned = outweight.T
    both = lax.all_gather(jnp.stack([queryweight, out_turned]), "tensor", axis=0)
    query_rows = both[:, 0].transpose(1, 0, 2).reshape(depth, n_tensor * width)
    out_rows = both[:, 1].transpose(1, 0, 2).reshape(depth, n_tensor * width)
    first_rows = jnp.concatenate([query_rows, keyvalue], axis=1)

    def whole(block):
        parts = ring.gather(block)
        full = jnp.zeros((n_dp * block.shape[0], block.shape[1]), block.dtype)
        for key in order:
            at = ring.owner(dp_index, *key) * block.shape[0]
            full = lax.dynamic_update_slice_in_dim(full, parts[key], at, 0)
        return full

    first_full = whole(first_rows)
    out_full = whole(out_rows)

    hidden_own = upweight.shape[1] // n_dp

    def hidden_slice(turned):
        mine = lax.all_to_all(turned, "dp", 0, 1, tiled=True)
        return lax.all_gather(mine, "tensor", axis=0, tiled=True)

    up_turned = hidden_slice(upweight.T)
    down_full = hidden_slice(downweight)
    bias_part = lax.dynamic_slice_in_dim(upbias, dp_index * hidden_own, hidden_own)
    biases = lax.all_gather(jnp.concatenate([querybias, bias_part]), "tensor", axis=0)
    query_shift = biases[:, :width].reshape(-1)
    up_shift = biases[:, width:].reshape(-1)

    first_mean, first_scale = norm_stats(rows)
    normed_first = ((rows - first_mean) * first_scale * attngain + attnshift).astype(bf16)
    shift = jnp.concatenate([query_shift, jnp.zeros((head_dim,), f32), valuebias])
    qkv = (dot_nn(normed_first, first_full) + shift).astype(bf16)
    kv_all = lax.all_gather(qkv[:, model:], "tensor", axis=0, tiled=True)

    keys = 256 if length % 256 == 0 else 128
    query_block = min(128, count)
    first_row = tensor_index * count
    own_segment = lax.dynamic_slice_in_dim(segment, first_row, count)
    starts = jnp.sum(
        (segment[None, :] < own_segment[:, None]).astype(jnp.int32), axis=1
    )
    block_first = first_row + jnp.arange(count // query_block, dtype=jnp.int32) * query_block
    info = jnp.stack(
        [
            starts[::query_block] // keys,
            (block_first + query_block - 1) // keys + 1,
            block_first,
        ]
    ).astype(jnp.int32)
    starts = starts.reshape(1, count)
    mixed, totals = attend_forward(qkv, kv_all, info, starts, head_dim, keys)
    residual = rows + dot_nt(mixed, out_full) + outbias
    second_mean, second_scale = norm_stats(residual)
    normed_second = ((residual - second_mean) * second_scale * mlpgain + mlpshift).astype(bf16)

    grads = ring.gather(cotangent)
    seconds = ring.gather(normed_second)
    active, grad_pre = {}, {}
    for key in order:
        preact = dot_nt(seconds[key], up_turned) + up_shift
        value, slope = gelu_both(preact)
        active[key] = value.astype(bf16)
        grad_pre[key] = (dot_nt(grads[key], down_full) * slope).astype(bf16)
    grad_second = ring.scatter_sum(lambda o, c: dot_nn(grad_pre[(o, c)], up_turned))
    second_out = ring.scatter_sum(lambda o, c: dot_nn(active[(o, c)], down_full))
    layer_out = residual + second_out + downbias

    def joined(parts):
        return jnp.concatenate([parts[key] for key in order], axis=0)

    pre_all = joined(grad_pre)
    upbias_part = jnp.sum(pre_all.astype(f32), axis=0)
    up_local = dot_tn(pre_all, joined(seconds))
    down_local = dot_tn(joined(active), joined(grads))

    def hidden_owner(local):
        part = lax.psum_scatter(local.astype(bf16), "tensor", scatter_dimension=0, tiled=True)
        return lax.all_to_all(part, "dp", 1, 0, tiled=True).astype(f32)

    down_grad = hidden_owner(down_local)
    up_grad = hidden_owner(up_local).T

    grad_out = cotangent.astype(f32)
    grad_two, mlpgain_part, mlpshift_part = norm_backward(
        residual, second_mean, second_scale, mlpgain, grad_second
    )
    grad_resid = grad_out + grad_two
    grad_branch = grad_resid.astype(bf16)
    grad_mixed = dot_nn(grad_branch, out_full).astype(bf16)
    grad_queries, grad_kv = attend_backward(
        qkv, grad_mixed, mixed, kv_all, info, starts, totals, head_dim, keys
    )
    grad_pairs = lax.psum_scatter(grad_kv, "tensor", scatter_dimension=0, tiled=True).astype(bf16)
    grad_qkv = jnp.concatenate([grad_queries, grad_pairs], axis=1)
    grad_first = dot_nt(grad_qkv, first_full)
    grad_one, attngain_part, attnshift_part = norm_backward(
        rows, first_mean, first_scale, attngain, grad_first
    )
    tokens_grad = (grad_resid + grad_one).astype(bf16)

    def depth_owner(local):
        def part(offset, other):
            at = ring.owner(dp_index, offset, other) * depth
            return lax.dynamic_slice_in_dim(local, at, depth, 0)

        return ring.scatter_sum(part)

    def width_owner(block):
        parts = block.astype(bf16).reshape(depth, n_tensor, width).transpose(1, 0, 2)
        return lax.psum_scatter(parts, "tensor", scatter_dimension=0, tiled=False).astype(f32)

    out_grad = width_owner(depth_owner(dot_tn(grad_branch, mixed))).T
    first_part = depth_owner(dot_tn(normed_first, grad_qkv))
    query_grad = width_owner(first_part[:, :model])
    pair_part = lax.all_gather(first_part[:, model:], "tensor", axis=0)
    keyvalue_grad = jnp.sum(pair_part, axis=0)

    shift_part = jnp.sum(grad_qkv.astype(f32), axis=0)
    vectors = [
        attngain_part,
        attnshift_part,
        mlpgain_part,
        mlpshift_part,
        jnp.sum(grad_branch.astype(f32), axis=0),
        jnp.sum(grad_out, axis=0),
        shift_part[:model],
        shift_part[model + head_dim :],
        upbias_part,
    ]
    sizes = [v.shape[0] for v in vectors]
    over_tensor = jnp.sum(lax.all_gather(jnp.concatenate(vectors), "tensor", axis=0), axis=0)
    plain = sum(sizes[:-1])
    up_own = lax.dynamic_slice_in_dim(
        over_tensor, plain + tensor_index * hidden_own, hidden_own
    )
    gathered = lax.all_gather(
        jnp.concatenate([over_tensor[:plain], up_own]), "dp", axis=0
    )
    summed = jnp.sum(gathered[:, :plain], axis=0)
    upbias_grad = gathered[:, plain:].reshape(-1)
    found = []
    at = 0
    for size in sizes[:-1]:
        found.append(summed[at : at + size])
        at += size
    querybias_grad = lax.dynamic_slice_in_dim(found[6], tensor_index * width, width)
    return (
        layer_out.astype(bf16),
        tokens_grad,
        found[0],
        found[1],
        query_grad,
        querybias_grad,
        keyvalue_grad,
        found[7],
        out_grad,
        found[4],
        found[2],
        found[3],
        up_grad,
        upbias_grad,
        down_grad,
        found[5],
    )


def solution(mesh):
    return jax.shard_map(
        on_device,
        mesh=mesh,
        in_specs=(
            P(("dp", "tensor"), None),
            P("dp", None),
            P(),
            P(),
            P("dp", "tensor"),
            P("tensor"),
            P("dp", None),
            P(),
            P("tensor", "dp"),
            P(),
            P(),
            P(),
            P("dp", "tensor"),
            P("tensor"),
            P("tensor", "dp"),
            P(),
            P(("dp", "tensor"), None),
        ),
        out_specs=(
            P(("dp", "tensor"), None),
            P(("dp", "tensor"), None),
            P(),
            P(),
            P("dp", "tensor"),
            P("tensor"),
            P("dp", None),
            P(),
            P("tensor", "dp"),
            P(),
            P(),
            P(),
            P("dp", "tensor"),
            P("tensor"),
            P("tensor", "dp"),
            P(),
        ),
        check_vma=False,
    )
```

```python
import functools

import jax
import jax.numpy as jnp
from jax import lax
from jax.experimental import pallas as pl
from jax.experimental.pallas import tpu as pltpu
from jax.sharding import PartitionSpec as P

eps_norm = 1e-05
masked_score = -1e30
log2_e = 1.4426950408889634
bf16 = jnp.bfloat16
f32 = jnp.float32


def dot_nn(left_side, right_side):
    return jnp.dot(left_side, right_side, preferred_element_type=f32)


def dot_tn(left_side, right_side):
    return lax.dot_general(
        left_side, right_side, (((0,), (0,)), ((), ())), preferred_element_type=f32
    )


def dot_nt(left_side, right_side):
    return lax.dot_general(
        left_side, right_side, (((1,), (1,)), ((), ())), preferred_element_type=f32
    )


def norm_stats(values):
    row_mean = jnp.mean(values, axis=-1, keepdims=True)
    centered = values - row_mean
    row_var = jnp.mean(centered * centered, axis=-1, keepdims=True)
    scale = lax.rsqrt(row_var + eps_norm)
    return row_mean, scale


def norm_backward(values, row_mean, scale, gain, grad):
    xhat = (values - row_mean) * scale
    u = grad * gain
    u_mean = jnp.mean(u, axis=-1, keepdims=True)
    ux_mean = jnp.mean(u * xhat, axis=-1, keepdims=True)
    grad_in = (u - u_mean - xhat * ux_mean) * scale
    return grad_in, jnp.sum(grad * xhat, axis=0), jnp.sum(grad, axis=0)


def norm_backward_kernel(
    one_ref, two_ref, three_ref, values_ref, out_ref, gain_ref, resid_ref, branch_ref, sums_ref
):
    grad = one_ref[...].astype(f32) + two_ref[...].astype(f32) + three_ref[...].astype(f32)
    values = values_ref[...]
    grad_out = out_ref[...].astype(f32)
    mean, scale = norm_stats(values)
    xhat = (values - mean) * scale
    u = grad * gain_ref[...]
    u_mean = jnp.mean(u, axis=-1, keepdims=True)
    ux_mean = jnp.mean(u * xhat, axis=-1, keepdims=True)
    resid = grad_out + (u - u_mean - xhat * ux_mean) * scale
    branch = resid.astype(bf16)
    resid_ref[...] = resid
    branch_ref[...] = branch

    @pl.when(pl.program_id(0) == 0)
    def _():
        sums_ref[...] = jnp.zeros_like(sums_ref)

    for k, rows in enumerate((grad * xhat, grad, branch.astype(f32), grad_out)):
        sums_ref[k : k + 1] += jnp.sum(rows, axis=0, keepdims=True)


def norm_backward_shares(shares, values, grad_out, gain):
    count, model = values.shape
    rows = min(128, count)
    tile = pl.BlockSpec((rows, model), lambda i: (i, 0))
    return pl.pallas_call(
        norm_backward_kernel,
        grid=(count // rows,),
        in_specs=[tile] * 5 + [pl.BlockSpec((1, model), lambda i: (0, 0))],
        out_specs=[tile, tile, pl.BlockSpec((8, model), lambda i: (0, 0))],
        out_shape=[
            jax.ShapeDtypeStruct((count, model), f32),
            jax.ShapeDtypeStruct((count, model), bf16),
            jax.ShapeDtypeStruct((8, model), f32),
        ],
        name="norm_backward",
    )(*shares, values, grad_out, gain.reshape(1, model))


gelu_c = 0.7978845608028654


def gelu_both(v):
    square = v * v
    inner = gelu_c * v * (1.0 + 0.044715 * square)
    t = jnp.tanh(inner)
    half = 0.5 * (1.0 + t)
    value = v * half
    slope = half + 0.5 * v * (1.0 - t * t) * (gelu_c * (1.0 + 3.0 * 0.044715 * square))
    return value, slope


def stack_heads(block, heads, width):
    return jnp.concatenate(
        [block[:, h * width : (h + 1) * width] for h in range(heads)], axis=0
    )


def block_bias(first_key, keys, start_row, query_row):
    key_at = first_key + lax.broadcasted_iota(jnp.int32, (keys, start_row.shape[1]), 0)
    allowed = (key_at >= start_row) & (key_at <= query_row)
    return jnp.where(allowed, 0.0, masked_score)


def attend_forward_kernel(
    heads, width, keys, info_ref, q_ref, kv_ref, start_ref, o_ref, total_ref
):
    at = pl.program_id(1)
    rows = q_ref.shape[0]
    q = stack_heads(q_ref[...], heads, width)
    start_row = start_ref[...]
    query_row = info_ref[2, at] + lax.broadcasted_iota(jnp.int32, (1, rows), 1)
    scale = width**-0.5 * log2_e

    def step(block, carried):
        top, total, mixed = carried
        first_key = pl.multiple_of(block * keys, keys)
        k = kv_ref[pl.ds(first_key, keys), :width]
        v = kv_ref[pl.ds(first_key, keys), width:]
        bias = block_bias(first_key, keys, start_row, query_row)
        scores = dot_nt(k, q) * scale + jnp.concatenate([bias] * heads, axis=1)
        new_top = jnp.maximum(top, jnp.max(scores, axis=0, keepdims=True))
        shrink = jnp.exp2(top - new_top)
        part = jnp.exp2(scores - new_top)
        total = total * shrink + jnp.sum(part, axis=0, keepdims=True)
        mixed = mixed * shrink + dot_tn(v, part.astype(bf16))
        return new_top, total, mixed

    count = heads * rows
    top, total, mixed = lax.fori_loop(
        info_ref[0, at],
        info_ref[1, at],
        step,
        (
            jnp.full((1, count), masked_score, f32),
            jnp.zeros((1, count), f32),
            jnp.zeros((width, count), f32),
        ),
    )
    out = (mixed / total).T.astype(bf16)
    for h in range(heads):
        o_ref[:, h * width : (h + 1) * width] = out[h * rows : (h + 1) * rows]
    total_ref[...] = (top + jnp.log2(total)).reshape(total_ref.shape)


def attend_backward_kernel(
    heads,
    width,
    keys,
    info_ref,
    q_ref,
    grad_ref,
    o_ref,
    kv_ref,
    start_ref,
    total_ref,
    dq_ref,
    dkv_ref,
):
    at = pl.program_id(1)
    rows = q_ref.shape[0]

    @pl.when((pl.program_id(0) == 0) & (at == 0))
    def _():
        dkv_ref[...] = jnp.zeros_like(dkv_ref)

    q = stack_heads(q_ref[...], heads, width)
    grad = stack_heads(grad_ref[...], heads, width)
    out = stack_heads(o_ref[...], heads, width)
    delta = jnp.sum((grad.astype(f32) * out.astype(f32)).T, axis=0, keepdims=True)
    count = heads * rows
    total = total_ref[...].reshape(1, count)
    start_row = start_ref[...]
    query_row = info_ref[2, at] + lax.broadcasted_iota(jnp.int32, (1, rows), 1)
    scale = width**-0.5

    def step(block, dq):
        first_key = pl.multiple_of(block * keys, keys)
        k = kv_ref[pl.ds(first_key, keys), :width]
        v = kv_ref[pl.ds(first_key, keys), width:]
        bias = block_bias(first_key, keys, start_row, query_row)
        scores = dot_nt(k, q) * (scale * log2_e) + jnp.concatenate([bias] * heads, axis=1)
        probs = jnp.exp2(scores - total)
        dprobs = dot_nt(v, grad)
        dscores = (probs * (dprobs - delta)).astype(bf16)
        dkv_ref[pl.ds(first_key, keys), :width] += dot_nn(dscores, q) * scale
        dkv_ref[pl.ds(first_key, keys), width:] += dot_nn(probs.astype(bf16), grad)
        return dq + dot_tn(k, dscores)

    dq = lax.fori_loop(
        info_ref[0, at], info_ref[1, at], step, jnp.zeros((width, count), f32)
    )
    dq = (dq * scale).T.astype(bf16)
    for h in range(heads):
        dq_ref[:, h * width : (h + 1) * width] = dq[h * rows : (h + 1) * rows]


def attend_shapes(queries, width):
    tokens = queries.shape[0]
    heads_all = queries.shape[1] // width
    heads = 16 if heads_all % 16 == 0 else heads_all
    rows = min(128, tokens)
    return tokens, heads_all, heads, heads_all // heads, rows, tokens // rows


def attend_forward(queries, kv_all, info, starts, width, keys):
    tokens, heads_all, heads, groups, rows, blocks = attend_shapes(queries, width)
    return pl.pallas_call(
        functools.partial(attend_forward_kernel, heads, width, keys),
        grid_spec=pltpu.PrefetchScalarGridSpec(
            num_scalar_prefetch=1,
            grid=(groups, blocks),
            in_specs=[
                pl.BlockSpec((rows, heads * width), lambda g, i, info: (i, g)),
                pl.BlockSpec(kv_all.shape, lambda g, i, info: (0, 0)),
                pl.BlockSpec((1, rows), lambda g, i, info: (0, i)),
            ],
            out_specs=[
                pl.BlockSpec((rows, heads * width), lambda g, i, info: (i, g)),
                pl.BlockSpec((1, 1, 1, heads * rows), lambda g, i, info: (g, i, 0, 0)),
            ],
        ),
        out_shape=[
            jax.ShapeDtypeStruct((tokens, heads_all * width), bf16),
            jax.ShapeDtypeStruct((groups, blocks, 1, heads * rows), f32),
        ],
        name="attend_forward",
    )(info, queries, kv_all, starts)


def attend_backward(queries, grad, mixed, kv_all, info, starts, totals, width, keys):
    tokens, heads_all, heads, groups, rows, blocks = attend_shapes(queries, width)
    tile = pl.BlockSpec((rows, heads * width), lambda g, i, info: (i, g))
    return pl.pallas_call(
        functools.partial(attend_backward_kernel, heads, width, keys),
        grid_spec=pltpu.PrefetchScalarGridSpec(
            num_scalar_prefetch=1,
            grid=(groups, blocks),
            in_specs=[
                tile,
                tile,
                tile,
                pl.BlockSpec(kv_all.shape, lambda g, i, info: (0, 0)),
                pl.BlockSpec((1, rows), lambda g, i, info: (0, i)),
                pl.BlockSpec((1, 1, 1, heads * rows), lambda g, i, info: (g, i, 0, 0)),
            ],
            out_specs=[
                tile,
                pl.BlockSpec(kv_all.shape, lambda g, i, info: (0, 0)),
            ],
        ),
        out_shape=[
            jax.ShapeDtypeStruct((tokens, heads_all * width), bf16),
            jax.ShapeDtypeStruct(kv_all.shape, f32),
        ],
        name="attend_backward",
    )(info, queries, grad, mixed, kv_all, starts, totals)


def after(value, *earlier):
    return lax.optimization_barrier((value, earlier))[0]


def axis_gather(block, axis):
    copies = jnp.broadcast_to(block[None], (lax.axis_size(axis),) + block.shape)
    return lax.all_to_all(copies, axis, 0, 0)


def tensor_exchange(parts, rows):
    parts = parts.reshape(lax.axis_size("tensor"), rows, parts.shape[1])
    return lax.all_to_all(parts, "tensor", 0, 0)


def tensor_swaps(parts):
    size = lax.axis_size("tensor")
    index = lax.axis_index("tensor")
    found = jnp.zeros(parts.shape, parts.dtype)
    zeros = (0,) * (parts.ndim - 1)
    for s in range(size):
        part = lax.dynamic_index_in_dim(parts, (index + s) % size, 0)
        if s:
            part = lax.ppermute(part, "tensor", [(i, (i + s) % size) for i in range(size)])
        found = lax.dynamic_update_slice(found, part, ((index - s) % size,) + zeros)
    return found


class Ring:
    def __init__(self, size):
        self.size = size
        self.chips = size // 2
        half = self.chips // 2
        if half:
            self.order = list(range(half)) + list(range(self.chips - 1, half - 1, -1))
        else:
            self.order = [0]
        n = self.chips
        self.pairs = []
        for i in range(n):
            here, there = self.order[i], self.order[(i + 1) % n]
            self.pairs += [(2 * here, 2 * there), (2 * there + 1, 2 * here + 1)]
        self.swap_pairs = [(i, i ^ 1) for i in range(size)]
        self.keys = [(s, c) for s in range(n) for c in (0, 1)]

    def owner(self, index, s, c):
        place = [0] * self.chips
        for i, chip in enumerate(self.order):
            place[chip] = i
        at = jnp.array(place, jnp.int32)[index // 2]
        core = index % 2 if c == 0 else 1 - index % 2
        at = (at + jnp.where(core == 0, -s, s)) % self.chips
        return 2 * jnp.array(self.order, jnp.int32)[at] + core

    def step(self, value):
        return lax.ppermute(value, "dp", self.pairs)

    def swap(self, value):
        return lax.ppermute(value, "dp", self.swap_pairs)

    def gather(self, own, gates=()):
        blocks = {(0, 0): own, (0, 1): self.swap(own)}
        for s in range(1, self.chips):
            if s < len(gates) and gates[s] is not None:
                own = after(own, gates[s])
            own = self.step(own)
            blocks[(s, 0)] = own
            blocks[(s, 1)] = self.swap(own)
        return blocks

    def sums(self, parts):
        held = None
        gate = yield
        for s in list(range(1, self.chips)) + [0]:
            there = self.swap(parts[(s, 1)].astype(bf16))
            if gate is not None:
                there = after(there, gate)
            shares = [parts[(s, 0)], there] + ([] if held is None else [held])
            if s:
                value = total(shares).astype(bf16)
                held = self.step(value)
                gate = yield value
            else:
                gate = yield shares


def total(shares):
    return sum(share.astype(f32) for share in shares)


def started(sums):
    next(sums)
    return sums


def units_kernel(count, piece, tiles, *refs):
    seconds, grads = refs[:count], refs[count : 2 * count]
    rows_ref, cols_ref, shift_ref = refs[2 * count : 2 * count + 3]
    outs = refs[2 * count + 3 :]
    actives, pres, shares, lasts = (outs[k * count : (k + 1) * count] for k in range(4))
    active_kept, pre_kept = (outs[k * count : (k + 1) * count] for k in (4, 5))
    at = pl.program_id(0)

    def pieces(block, first):
        width = block.shape[1]
        return jnp.concatenate(
            [block[:, k : k + piece] for k in range(first * piece, width, 2 * piece)], axis=1
        )

    @pl.when(at < tiles)
    def _():
        up, down = pieces(rows_ref, 0), pieces(rows_ref, 1)
        for k in range(count):
            preact = dot_nt(seconds[k][...], up) + shift_ref[...]
            grad_active = dot_nt(grads[k][...], down)
            value, slope = gelu_both(preact)
            value = value.astype(bf16)
            pre = (grad_active * slope).astype(bf16)
            actives[k][...] = value
            pres[k][...] = pre
            active_kept[k][at] = value
            pre_kept[k][at] = pre

    @pl.when(at >= tiles)
    def _():
        up, down = pieces(cols_ref, 0), pieces(cols_ref, 1)
        for k in range(count):
            pre = jnp.concatenate([pre_kept[k][j] for j in range(tiles)], axis=1)
            shares[k][...] = dot_nn(pre, up).astype(bf16)
            value = jnp.concatenate([active_kept[k][j] for j in range(tiles)], axis=1)
            lasts[k][...] = dot_nn(value, down).astype(bf16)


def units(seconds, grads, weights, piece, shift):
    count = len(seconds)
    rows, model = seconds[0].shape
    hidden = weights.shape[0]
    width = min(256, hidden)
    tiles = hidden // width
    turns = model // (2 * piece)
    tile = pl.BlockSpec((rows, width), lambda j: (0, jnp.minimum(j, tiles - 1)))
    whole = pl.BlockSpec((rows, model), lambda j: (0, 0))
    part = pl.BlockSpec((rows, 2 * piece), lambda j: (0, jnp.maximum(j - tiles, 0)))
    out = pl.pallas_call(
        functools.partial(units_kernel, count, piece, tiles),
        grid=(tiles + turns,),
        in_specs=[whole] * (2 * count)
        + [
            pl.BlockSpec((width, 2 * model), lambda j: (jnp.minimum(j, tiles - 1), 0)),
            pl.BlockSpec((hidden, 4 * piece), lambda j: (0, jnp.maximum(j - tiles, 0))),
            pl.BlockSpec((1, width), lambda j: (0, jnp.minimum(j, tiles - 1))),
        ],
        out_specs=[tile] * (2 * count) + [part] * (2 * count),
        out_shape=[jax.ShapeDtypeStruct((rows, hidden), bf16)] * (2 * count)
        + [jax.ShapeDtypeStruct((rows, model), bf16)] * (2 * count),
        scratch_shapes=[pltpu.VMEM((tiles, rows, width), bf16)] * (2 * count),
        cost_estimate=pl.CostEstimate(
            flops=8 * count * rows * model * hidden,
            transcendentals=count * rows * hidden,
            bytes_accessed=8 * hidden * model + 4 * count * rows * (2 * model + hidden),
        ),
        name="units",
    )(*seconds, *grads, weights, weights, shift.reshape(1, hidden))
    return [out[k * count : (k + 1) * count] for k in range(4)]


def rows_product_kernel(depth, owner_ref, left_ref, shift_ref, *refs):
    blocks, out_ref = refs[:-1], refs[-1]
    total = jnp.broadcast_to(shift_ref[...], out_ref.shape)
    for k, block in enumerate(blocks):
        at = pl.multiple_of(owner_ref[k] * depth, depth)
        total = total + dot_nn(left_ref[:, pl.ds(at, depth)], block[...])
    out_ref[...] = total.astype(out_ref.dtype)


def rows_product(left, blocks, owners, shift):
    depth, width = blocks[0].shape
    tile = 128 * max(t for t in range(1, 9) if width % (128 * t) == 0)
    return pl.pallas_call(
        functools.partial(rows_product_kernel, depth),
        grid_spec=pltpu.PrefetchScalarGridSpec(
            num_scalar_prefetch=1,
            grid=(width // tile,),
            in_specs=[
                pl.BlockSpec(left.shape, lambda j, owner: (0, 0)),
                pl.BlockSpec((1, tile), lambda j, owner: (0, j)),
            ]
            + [pl.BlockSpec((depth, tile), lambda j, owner: (0, j)) for _ in blocks],
            out_specs=pl.BlockSpec((left.shape[0], tile), lambda j, owner: (0, j)),
        ),
        out_shape=jax.ShapeDtypeStruct((left.shape[0], width), bf16),
        cost_estimate=pl.CostEstimate(
            flops=2 * left.shape[0] * left.shape[1] * width,
            transcendentals=0,
            bytes_accessed=2 * left.shape[1] * width,
        ),
        name="rows_product",
    )(owners, left, shift.reshape(1, width), *blocks)


def grads_product_kernel(count, *refs):
    out_ref, sum_ref = refs[2 * count :]
    total = dot_tn(refs[0][...], refs[count][...])
    for k in range(1, count):
        total = total + dot_tn(refs[k][...], refs[count + k][...])
    out_ref[...] = total.astype(out_ref.dtype)

    @pl.when(pl.program_id(0) == 0)
    def _():
        sums = jnp.zeros(sum_ref.shape, f32)
        for k in range(count):
            sums = sums + jnp.sum(refs[k][...].astype(f32), axis=0, keepdims=True)
        sum_ref[...] = sums


def grads_product(lefts, rights):
    rows, units = lefts[0].shape
    width = rights[0].shape[1]
    tile = min(512, width)
    count = len(lefts)
    return pl.pallas_call(
        functools.partial(grads_product_kernel, count),
        grid=(width // tile,),
        in_specs=[pl.BlockSpec((rows, units), lambda j: (0, 0)) for _ in lefts]
        + [pl.BlockSpec((rows, tile), lambda j: (0, j)) for _ in rights],
        out_specs=[
            pl.BlockSpec((units, tile), lambda j: (0, j)),
            pl.BlockSpec((1, units), lambda j: (0, 0)),
        ],
        out_shape=[
            jax.ShapeDtypeStruct((units, width), bf16),
            jax.ShapeDtypeStruct((1, units), f32),
        ],
        cost_estimate=pl.CostEstimate(
            flops=2 * count * rows * units * width,
            transcendentals=0,
            bytes_accessed=2 * count * rows * (units + width) + 2 * units * width,
        ),
        name="grads_product",
    )(*lefts, *rights)


def cols_product_kernel(depth, owner_ref, left_ref, *refs):
    blocks, out_ref = refs[:-1], refs[-1]
    left = left_ref[...]
    for k, block in enumerate(blocks):
        at = pl.multiple_of(owner_ref[k] * depth, depth)
        out_ref[:, pl.ds(at, depth)] = dot_nt(left, block[...])


def cols_product(left, blocks, owners):
    depth, width = blocks[0].shape
    rows = left.shape[0]
    out_width = depth * len(blocks)
    return pl.pallas_call(
        functools.partial(cols_product_kernel, depth),
        grid_spec=pltpu.PrefetchScalarGridSpec(
            num_scalar_prefetch=1,
            grid=(left.shape[0] // rows,),
            in_specs=[pl.BlockSpec((rows, width), lambda i, owner: (i, 0))]
            + [pl.BlockSpec((depth, width), lambda i, owner: (0, 0)) for _ in blocks],
            out_specs=pl.BlockSpec((rows, out_width), lambda i, owner: (i, 0)),
        ),
        out_shape=jax.ShapeDtypeStruct((left.shape[0], out_width), f32),
        cost_estimate=pl.CostEstimate(
            flops=2 * left.shape[0] * out_width * width,
            transcendentals=0,
            bytes_accessed=2 * out_width * width,
        ),
        name="cols_product",
    )(owners, left, *blocks)


def on_device(
    tokens,
    segment_ids,
    attngain,
    attnshift,
    queryweight,
    querybias,
    keyvalue,
    valuebias,
    outweight,
    outbias,
    mlpgain,
    mlpshift,
    upweight,
    upbias,
    downweight,
    downbias,
    cotangent,
):
    head_dim = valuebias.shape[0]
    count, model = tokens.shape
    n_dp = lax.axis_size("dp")
    n_tensor = lax.axis_size("tensor")
    dp_index = lax.axis_index("dp")
    tensor_index = lax.axis_index("tensor")
    ring = Ring(n_dp)
    order = ring.keys
    owners = jnp.stack([ring.owner(dp_index, *key) for key in order]).astype(jnp.int32)
    segment = segment_ids[0]
    length = segment.shape[0]
    rows = tokens.astype(f32)
    depth = queryweight.shape[0]
    width = queryweight.shape[1]

    both = lax.all_gather(jnp.stack([queryweight, outweight.T]), "tensor", axis=0)
    both = both.transpose(1, 2, 0, 3).reshape(2, depth, n_tensor * width)

    hidden_own = upweight.shape[1] // n_dp
    bias_part = lax.dynamic_slice_in_dim(upbias, dp_index * hidden_own, hidden_own)
    biases = axis_gather(jnp.concatenate([querybias, bias_part]), "tensor")
    query_shift = biases[:, :width].reshape(-1)
    up_shift = biases[:, width:].reshape(-1)
    pair_full = axis_gather(after(keyvalue, biases), "dp").reshape(model, 2 * head_dim)

    first_mean, first_scale = norm_stats(rows)
    normed_first = ((rows - first_mean) * first_scale * attngain + attnshift).astype(bf16)
    pair_shift = jnp.concatenate([jnp.zeros((head_dim,), f32), valuebias])
    pairs = (dot_nn(normed_first, pair_full) + pair_shift).astype(bf16)

    weights = after(jnp.concatenate([upweight.T, downweight], axis=1), pair_full)
    weights = lax.all_to_all(weights, "dp", 0, 1, tiled=True)
    kv_all = axis_gather(after(pairs, weights), "tensor").reshape(length, 2 * head_dim)

    first_blocks = ring.gather(both[0], (None, None, weights, kv_all))
    first_list = [first_blocks[key] for key in order]
    weights = lax.all_gather(after(weights, kv_all), "tensor", axis=0, tiled=True)

    grads = {(0, 0): cotangent, (1, 0): ring.step(cotangent)}
    normed_late = after(normed_first, grads[(1, 0)])
    queries = rows_product(normed_late, first_list, owners, query_shift)
    if ring.chips > 2:
        grads[(2, 0)] = ring.step(after(grads[(1, 0)], queries))
    keys = 256 if length % 256 == 0 else 128
    query_block = min(128, count)
    first_row = tensor_index * count
    own_segment = lax.dynamic_slice_in_dim(segment, first_row, count)
    starts = jnp.sum(
        (segment[None, :] < own_segment[:, None]).astype(jnp.int32), axis=1
    )
    block_first = first_row + jnp.arange(count // query_block, dtype=jnp.int32) * query_block
    info = jnp.stack(
        [
            starts[::query_block] // keys,
            (block_first + query_block - 1) // keys + 1,
            block_first,
        ]
    ).astype(jnp.int32)
    starts = starts.reshape(1, count)
    mixed, totals = attend_forward(queries, kv_all, info, starts, head_dim, keys)
    for at in range(3, ring.chips):
        grads[(at, 0)] = ring.step(after(grads[(at - 1, 0)], mixed))
    for at in range(ring.chips):
        grads[(at, 1)] = ring.swap(after(grads[(at, 0)], mixed))
    out_blocks = ring.gather(both[1], (None, first_list, queries, mixed))
    out_list = [out_blocks[key] for key in order]
    residual = rows + cols_product(after(mixed, grads[(min(2, ring.chips - 1), 0)]), out_list, owners) + outbias
    second_mean, second_scale = norm_stats(residual)
    normed_second = ((residual - second_mean) * second_scale * mlpgain + mlpshift).astype(bf16)

    active, grad_pre, second_parts, last_parts, seconds = {}, {}, {}, {}, {}
    done = []

    def work(s):
        keys_here = [(s, 0), (s, 1)]
        seconds[keys_here[0]] = passed[s]
        seconds[keys_here[1]] = ring.swap(after(passed[s], done))
        found = units(
            [after(seconds[key], done[-1:]) for key in keys_here],
            [grads[key] for key in keys_here],
            weights,
            depth,
            up_shift,
        )
        done.append(found[2])
        for kept, values in zip((active, grad_pre, second_parts, last_parts), found):
            kept.update(zip(keys_here, values))

    passed = [normed_second]
    for s in range(1, ring.chips):
        if s >= 3:
            work(s - 2)
        passed.append(ring.step(after(passed[-1], done)))
    for s in range(max(1, ring.chips - 2), ring.chips):
        work(s)
    work(0)
    sums = started(ring.sums(second_parts))
    for at in range(ring.chips):
        grad_second = sums.send(done[min(at + 1, len(done) - 1)])
    parts_done = done[-1]
    up_local, upbias_part = grads_product(
        [after(grad_pre[key], parts_done) for key in order], [seconds[key] for key in order]
    )
    up_part = lax.psum_scatter(up_local, "tensor", scatter_dimension=0, tiled=True)
    grad_second = [after(share, up_local) for share in grad_second]
    grad_second += [jnp.zeros_like(cotangent)] * (3 - len(grad_second))

    grad_resid, grad_branch, second_sums = norm_backward_shares(
        grad_second, residual, cotangent, mlpgain
    )
    grad_mixed = rows_product(grad_branch, out_list, owners, jnp.zeros((model,), f32))
    grad_queries, grad_kv = attend_backward(
        queries, grad_mixed, mixed, kv_all, info, starts, totals, head_dim, keys
    )

    def depth_sums(local):
        return started(
            ring.sums(
                {
                    key: lax.dynamic_slice_in_dim(local, owners[k] * depth, depth, 0)
                    for k, key in enumerate(order)
                }
            )
        )

    def width_owner(block):
        parts = block.astype(bf16).reshape(depth, n_tensor, width).transpose(1, 0, 2)
        return lax.psum_scatter(parts, "tensor", scatter_dimension=0, tiled=False).astype(f32)

    chips = ring.chips
    last_sums = started(ring.sums(last_parts))
    last_sent = [last_sums.send(gate) for gate in (grad_mixed, grad_queries)[:chips]]
    pair_raw = tensor_exchange(grad_kv.astype(bf16), count)
    down_local, _ = grads_product(
        [after(active[key], grad_queries, last_sent) for key in order],
        [grads[key] for key in order],
    )
    down_part = lax.psum_scatter(down_local, "tensor", scatter_dimension=0, tiled=True)
    out_local = dot_tn(after(grad_branch, down_local), mixed).astype(bf16)
    out_sums = depth_sums(out_local)
    out_sent = [out_sums.send(None)]
    if chips > 2:
        last_sent.append(last_sums.send(down_local))
    pair_shares = after(pair_raw, down_local)
    grad_pairs = jnp.sum(pair_shares.astype(f32), axis=0).astype(bf16)
    grad_qkv = jnp.concatenate([grad_queries, grad_pairs], axis=1)
    first_local = dot_tn(normed_first, grad_qkv).astype(bf16)
    first_sums = depth_sums(first_local)
    first_sent = [first_sums.send(None) for _ in range(chips)]
    first_part = total(first_sent[-1])
    for at in range(1, chips):
        out_sent.append(out_sums.send(first_part))
    out_part = total(out_sent[-1])
    for at in range(len(last_sent), chips):
        last_sent.append(last_sums.send(first_part))
    layer_out = residual + total(last_sent[-1]) + downbias
    up_grad = lax.all_to_all(after(up_part, first_part), "dp", 1, 0, tiled=True).astype(f32).T
    grad_first = cols_product(after(grad_queries, first_sent[min(1, chips - 1)]), first_list, owners)
    grad_first = grad_first + dot_nt(grad_pairs, pair_full)
    grad_one, attngain_part, attnshift_part = norm_backward(
        rows, first_mean, first_scale, attngain, grad_first
    )
    tokens_grad = (grad_resid + grad_one).astype(bf16)

    shift_part = jnp.sum(grad_qkv.astype(f32), axis=0)
    vectors = [
        attngain_part,
        attnshift_part,
        second_sums[0],
        second_sums[1],
        second_sums[2],
        second_sums[3],
        shift_part[:model],
        shift_part[model + head_dim :],
    ]
    sizes = [v.shape[0] for v in vectors]
    plain = sum(sizes)
    flat = jnp.concatenate(vectors + [upbias_part[0]])
    flat = axis_gather(flat, "dp")
    units_flat = flat[:, plain:].reshape(n_dp, n_tensor, hidden_own)
    units_flat = units_flat.transpose(1, 0, 2).reshape(n_tensor, n_dp * hidden_own)
    flat = jnp.broadcast_to(jnp.sum(flat[:, :plain], axis=0), (n_tensor, plain))
    flat = lax.all_to_all(jnp.concatenate([flat, units_flat], axis=1), "tensor", 0, 0, tiled=True)
    flat = jnp.sum(flat, axis=0)

    first_sent = first_part.astype(bf16)
    first_sent = jnp.concatenate(
        [
            first_sent[:, :model].reshape(depth, n_tensor, width).transpose(1, 0, 2),
            jnp.broadcast_to(first_sent[None, :, model:], (n_tensor, depth, 2 * head_dim)),
        ],
        axis=2,
    )
    first_sent = tensor_swaps(first_sent)
    down_grad = lax.all_to_all(after(down_part, up_grad), "dp", 1, 0, tiled=True).astype(f32)
    out_grad = width_owner(after(out_part, first_sent)).T
    first_grad = jnp.sum(first_sent.astype(f32), axis=0)
    query_grad = first_grad[:, :width]
    keyvalue_grad = first_grad[:, width:]

    upbias_grad = flat[plain : plain + n_dp * hidden_own]
    found = []
    at = 0
    for size in sizes:
        found.append(flat[at : at + size])
        at += size
    attngain_grad, attnshift_grad, mlpgain_grad, mlpshift_grad = found[:4]
    outbias_grad, downbias_grad, query_shift_grad, valuebias_grad = found[4:]
    querybias_grad = lax.dynamic_slice_in_dim(query_shift_grad, tensor_index * width, width)
    return (
        layer_out.astype(bf16),
        tokens_grad,
        attngain_grad,
        attnshift_grad,
        query_grad,
        querybias_grad,
        keyvalue_grad,
        valuebias_grad,
        out_grad,
        outbias_grad,
        mlpgain_grad,
        mlpshift_grad,
        up_grad,
        upbias_grad,
        down_grad,
        downbias_grad,
    )


def solution(mesh):
    return jax.shard_map(
        on_device,
        mesh=mesh,
        in_specs=(
            P(("dp", "tensor"), None),
            P("dp", None),
            P(),
            P(),
            P("dp", "tensor"),
            P("tensor"),
            P("dp", None),
            P(),
            P("tensor", "dp"),
            P(),
            P(),
            P(),
            P("dp", "tensor"),
            P("tensor"),
            P("tensor", "dp"),
            P(),
            P(("dp", "tensor"), None),
        ),
        out_specs=(
            P(("dp", "tensor"), None),
            P(("dp", "tensor"), None),
            P(),
            P(),
            P("dp", "tensor"),
            P("tensor"),
            P("dp", None),
            P(),
            P("tensor", "dp"),
            P(),
            P(),
            P(),
            P("dp", "tensor"),
            P("tensor"),
            P("tensor", "dp"),
            P(),
        ),
        check_vma=False,
    )
```

```python
import functools

import jax
import jax.numpy as jnp
from jax import lax
from jax.experimental import pallas as pl
from jax.experimental.pallas import tpu as pltpu
from jax.sharding import PartitionSpec as P

eps_norm = 1e-05
masked_score = -1e30
log2_e = 1.4426950408889634
bf16 = jnp.bfloat16
f32 = jnp.float32


def dot_nn(left_side, right_side):
    return jnp.dot(left_side, right_side, preferred_element_type=f32)


def dot_tn(left_side, right_side):
    return lax.dot_general(
        left_side, right_side, (((0,), (0,)), ((), ())), preferred_element_type=f32
    )


def dot_nt(left_side, right_side):
    return lax.dot_general(
        left_side, right_side, (((1,), (1,)), ((), ())), preferred_element_type=f32
    )


def norm_stats(values):
    row_mean = jnp.mean(values, axis=-1, keepdims=True)
    centered = values - row_mean
    row_var = jnp.mean(centered * centered, axis=-1, keepdims=True)
    scale = lax.rsqrt(row_var + eps_norm)
    return row_mean, scale


def norm_backward(values, row_mean, scale, gain, grad):
    xhat = (values - row_mean) * scale
    u = grad * gain
    u_mean = jnp.mean(u, axis=-1, keepdims=True)
    ux_mean = jnp.mean(u * xhat, axis=-1, keepdims=True)
    grad_in = (u - u_mean - xhat * ux_mean) * scale
    return grad_in, jnp.sum(grad * xhat, axis=0), jnp.sum(grad, axis=0)


def norm_backward_kernel(
    one_ref, two_ref, three_ref, values_ref, out_ref, gain_ref, resid_ref, branch_ref, sums_ref
):
    grad = one_ref[...].astype(f32) + two_ref[...].astype(f32) + three_ref[...].astype(f32)
    values = values_ref[...]
    grad_out = out_ref[...].astype(f32)
    mean, scale = norm_stats(values)
    xhat = (values - mean) * scale
    u = grad * gain_ref[...]
    u_mean = jnp.mean(u, axis=-1, keepdims=True)
    ux_mean = jnp.mean(u * xhat, axis=-1, keepdims=True)
    resid = grad_out + (u - u_mean - xhat * ux_mean) * scale
    branch = resid.astype(bf16)
    resid_ref[...] = resid
    branch_ref[...] = branch

    @pl.when(pl.program_id(0) == 0)
    def _():
        sums_ref[...] = jnp.zeros_like(sums_ref)

    for k, rows in enumerate((grad * xhat, grad, branch.astype(f32), grad_out)):
        sums_ref[k : k + 1] += jnp.sum(rows, axis=0, keepdims=True)


def norm_backward_shares(shares, values, grad_out, gain):
    count, model = values.shape
    rows = min(128, count)
    tile = pl.BlockSpec((rows, model), lambda i: (i, 0))
    return pl.pallas_call(
        norm_backward_kernel,
        grid=(count // rows,),
        in_specs=[tile] * 5 + [pl.BlockSpec((1, model), lambda i: (0, 0))],
        out_specs=[tile, tile, pl.BlockSpec((8, model), lambda i: (0, 0))],
        out_shape=[
            jax.ShapeDtypeStruct((count, model), f32),
            jax.ShapeDtypeStruct((count, model), bf16),
            jax.ShapeDtypeStruct((8, model), f32),
        ],
        name="norm_backward",
    )(*shares, values, grad_out, gain.reshape(1, model))


gelu_c = 0.7978845608028654


def gelu_both(v):
    square = v * v
    inner = gelu_c * v * (1.0 + 0.044715 * square)
    t = jnp.tanh(inner)
    half = 0.5 * (1.0 + t)
    value = v * half
    slope = half + 0.5 * v * (1.0 - t * t) * (gelu_c * (1.0 + 3.0 * 0.044715 * square))
    return value, slope


def stack_heads(block, heads, width):
    return jnp.concatenate(
        [block[:, h * width : (h + 1) * width] for h in range(heads)], axis=0
    )


def block_bias(first_key, keys, start_row, query_row):
    key_at = first_key + lax.broadcasted_iota(jnp.int32, (keys, start_row.shape[1]), 0)
    allowed = (key_at >= start_row) & (key_at <= query_row)
    return jnp.where(allowed, 0.0, masked_score)


def attend_forward_kernel(
    heads, width, keys, info_ref, q_ref, kv_ref, start_ref, o_ref, total_ref
):
    at = pl.program_id(1)
    rows = q_ref.shape[0]
    q = stack_heads(q_ref[...], heads, width)
    start_row = start_ref[...]
    query_row = info_ref[2, at] + lax.broadcasted_iota(jnp.int32, (1, rows), 1)
    scale = width**-0.5 * log2_e

    def step(block, carried):
        top, total, mixed = carried
        first_key = pl.multiple_of(block * keys, keys)
        k = kv_ref[pl.ds(first_key, keys), :width]
        v = kv_ref[pl.ds(first_key, keys), width:]
        bias = block_bias(first_key, keys, start_row, query_row)
        scores = dot_nt(k, q) * scale + jnp.concatenate([bias] * heads, axis=1)
        new_top = jnp.maximum(top, jnp.max(scores, axis=0, keepdims=True))
        shrink = jnp.exp2(top - new_top)
        part = jnp.exp2(scores - new_top)
        total = total * shrink + jnp.sum(part, axis=0, keepdims=True)
        mixed = mixed * shrink + dot_tn(v, part.astype(bf16))
        return new_top, total, mixed

    count = heads * rows
    top, total, mixed = lax.fori_loop(
        info_ref[0, at],
        info_ref[1, at],
        step,
        (
            jnp.full((1, count), masked_score, f32),
            jnp.zeros((1, count), f32),
            jnp.zeros((width, count), f32),
        ),
    )
    out = (mixed / total).T.astype(bf16)
    for h in range(heads):
        o_ref[:, h * width : (h + 1) * width] = out[h * rows : (h + 1) * rows]
    total_ref[...] = (top + jnp.log2(total)).reshape(total_ref.shape)


def attend_backward_kernel(
    heads,
    width,
    keys,
    info_ref,
    q_ref,
    grad_ref,
    o_ref,
    kv_ref,
    start_ref,
    total_ref,
    dq_ref,
    dkv_ref,
):
    at = pl.program_id(1)
    rows = q_ref.shape[0]

    @pl.when((pl.program_id(0) == 0) & (at == 0))
    def _():
        dkv_ref[...] = jnp.zeros_like(dkv_ref)

    q = stack_heads(q_ref[...], heads, width)
    grad = stack_heads(grad_ref[...], heads, width)
    out = stack_heads(o_ref[...], heads, width)
    delta = jnp.sum((grad.astype(f32) * out.astype(f32)).T, axis=0, keepdims=True)
    count = heads * rows
    total = total_ref[...].reshape(1, count)
    start_row = start_ref[...]
    query_row = info_ref[2, at] + lax.broadcasted_iota(jnp.int32, (1, rows), 1)
    scale = width**-0.5

    def step(block, dq):
        first_key = pl.multiple_of(block * keys, keys)
        k = kv_ref[pl.ds(first_key, keys), :width]
        v = kv_ref[pl.ds(first_key, keys), width:]
        bias = block_bias(first_key, keys, start_row, query_row)
        scores = dot_nt(k, q) * (scale * log2_e) + jnp.concatenate([bias] * heads, axis=1)
        probs = jnp.exp2(scores - total)
        dprobs = dot_nt(v, grad)
        dscores = (probs * (dprobs - delta)).astype(bf16)
        dkv_ref[pl.ds(first_key, keys), :width] += dot_nn(dscores, q) * scale
        dkv_ref[pl.ds(first_key, keys), width:] += dot_nn(probs.astype(bf16), grad)
        return dq + dot_tn(k, dscores)

    dq = lax.fori_loop(
        info_ref[0, at], info_ref[1, at], step, jnp.zeros((width, count), f32)
    )
    dq = (dq * scale).T.astype(bf16)
    for h in range(heads):
        dq_ref[:, h * width : (h + 1) * width] = dq[h * rows : (h + 1) * rows]


def attend_shapes(queries, width):
    tokens = queries.shape[0]
    heads_all = queries.shape[1] // width
    heads = 16 if heads_all % 16 == 0 else heads_all
    rows = min(128, tokens)
    return tokens, heads_all, heads, heads_all // heads, rows, tokens // rows


def attend_forward(queries, kv_all, info, starts, width, keys):
    tokens, heads_all, heads, groups, rows, blocks = attend_shapes(queries, width)
    return pl.pallas_call(
        functools.partial(attend_forward_kernel, heads, width, keys),
        grid_spec=pltpu.PrefetchScalarGridSpec(
            num_scalar_prefetch=1,
            grid=(groups, blocks),
            in_specs=[
                pl.BlockSpec((rows, heads * width), lambda g, i, info: (i, g)),
                pl.BlockSpec(kv_all.shape, lambda g, i, info: (0, 0)),
                pl.BlockSpec((1, rows), lambda g, i, info: (0, i)),
            ],
            out_specs=[
                pl.BlockSpec((rows, heads * width), lambda g, i, info: (i, g)),
                pl.BlockSpec((1, 1, 1, heads * rows), lambda g, i, info: (g, i, 0, 0)),
            ],
        ),
        out_shape=[
            jax.ShapeDtypeStruct((tokens, heads_all * width), bf16),
            jax.ShapeDtypeStruct((groups, blocks, 1, heads * rows), f32),
        ],
        name="attend_forward",
    )(info, queries, kv_all, starts)


def attend_backward(queries, grad, mixed, kv_all, info, starts, totals, width, keys):
    tokens, heads_all, heads, groups, rows, blocks = attend_shapes(queries, width)
    tile = pl.BlockSpec((rows, heads * width), lambda g, i, info: (i, g))
    return pl.pallas_call(
        functools.partial(attend_backward_kernel, heads, width, keys),
        grid_spec=pltpu.PrefetchScalarGridSpec(
            num_scalar_prefetch=1,
            grid=(groups, blocks),
            in_specs=[
                tile,
                tile,
                tile,
                pl.BlockSpec(kv_all.shape, lambda g, i, info: (0, 0)),
                pl.BlockSpec((1, rows), lambda g, i, info: (0, i)),
                pl.BlockSpec((1, 1, 1, heads * rows), lambda g, i, info: (g, i, 0, 0)),
            ],
            out_specs=[
                tile,
                pl.BlockSpec(kv_all.shape, lambda g, i, info: (0, 0)),
            ],
        ),
        out_shape=[
            jax.ShapeDtypeStruct((tokens, heads_all * width), bf16),
            jax.ShapeDtypeStruct(kv_all.shape, f32),
        ],
        name="attend_backward",
    )(info, queries, grad, mixed, kv_all, starts, totals)


def after(value, *earlier):
    return lax.optimization_barrier((value, earlier))[0]


def axis_gather(block, axis):
    copies = jnp.broadcast_to(block[None], (lax.axis_size(axis),) + block.shape)
    return lax.all_to_all(copies, axis, 0, 0)


def tensor_exchange(parts, rows):
    parts = parts.reshape(lax.axis_size("tensor"), rows, parts.shape[1])
    return lax.all_to_all(parts, "tensor", 0, 0)


def tensor_swaps(parts):
    size = lax.axis_size("tensor")
    index = lax.axis_index("tensor")
    found = jnp.zeros(parts.shape, parts.dtype)
    zeros = (0,) * (parts.ndim - 1)
    for s in range(size):
        part = lax.dynamic_index_in_dim(parts, (index + s) % size, 0)
        if s:
            part = lax.ppermute(part, "tensor", [(i, (i + s) % size) for i in range(size)])
        found = lax.dynamic_update_slice(found, part, ((index - s) % size,) + zeros)
    return found


class Ring:
    def __init__(self, size):
        self.size = size
        self.chips = size // 2
        half = self.chips // 2
        if half:
            self.order = list(range(half)) + list(range(self.chips - 1, half - 1, -1))
        else:
            self.order = [0]
        n = self.chips
        self.pairs = []
        for i in range(n):
            here, there = self.order[i], self.order[(i + 1) % n]
            self.pairs += [(2 * here, 2 * there), (2 * there + 1, 2 * here + 1)]
        self.swap_pairs = [(i, i ^ 1) for i in range(size)]
        self.keys = [(s, c) for s in range(n) for c in (0, 1)]

    def owner(self, index, s, c):
        place = [0] * self.chips
        for i, chip in enumerate(self.order):
            place[chip] = i
        at = jnp.array(place, jnp.int32)[index // 2]
        core = index % 2 if c == 0 else 1 - index % 2
        at = (at + jnp.where(core == 0, -s, s)) % self.chips
        return 2 * jnp.array(self.order, jnp.int32)[at] + core

    def step(self, value):
        return lax.ppermute(value, "dp", self.pairs)

    def swap(self, value):
        return lax.ppermute(value, "dp", self.swap_pairs)

    def gather(self, own, gates=()):
        blocks = {(0, 0): own, (0, 1): self.swap(own)}
        for s in range(1, self.chips):
            if s < len(gates) and gates[s] is not None:
                own = after(own, gates[s])
            own = self.step(own)
            blocks[(s, 0)] = own
            blocks[(s, 1)] = self.swap(own)
        return blocks

    def sums(self, parts):
        held = None
        gate = yield
        for s in list(range(1, self.chips)) + [0]:
            there = self.swap(parts[(s, 1)].astype(bf16))
            if gate is not None:
                there = after(there, gate)
            shares = [parts[(s, 0)], there] + ([] if held is None else [held])
            if s:
                value = total(shares).astype(bf16)
                held = self.step(value)
                gate = yield value
            else:
                gate = yield shares


def total(shares):
    return sum(share.astype(f32) for share in shares)


def started(sums):
    next(sums)
    return sums


def units_kernel(count, piece, tiles, *refs):
    seconds, grads = refs[:count], refs[count : 2 * count]
    rows_ref, cols_ref, shift_ref = refs[2 * count : 2 * count + 3]
    outs = refs[2 * count + 3 :]
    actives, pres, shares, lasts = (outs[k * count : (k + 1) * count] for k in range(4))
    active_kept, pre_kept = (outs[k * count : (k + 1) * count] for k in (4, 5))
    at = pl.program_id(0)

    def pieces(block, first):
        width = block.shape[1]
        return jnp.concatenate(
            [block[:, k : k + piece] for k in range(first * piece, width, 2 * piece)], axis=1
        )

    @pl.when(at < tiles)
    def _():
        up, down = pieces(rows_ref, 0), pieces(rows_ref, 1)
        for k in range(count):
            preact = dot_nt(seconds[k][...], up) + shift_ref[...]
            grad_active = dot_nt(grads[k][...], down)
            value, slope = gelu_both(preact)
            value = value.astype(bf16)
            pre = (grad_active * slope).astype(bf16)
            actives[k][...] = value
            pres[k][...] = pre
            active_kept[k][at] = value
            pre_kept[k][at] = pre

    @pl.when(at >= tiles)
    def _():
        up, down = pieces(cols_ref, 0), pieces(cols_ref, 1)
        for k in range(count):
            pre = jnp.concatenate([pre_kept[k][j] for j in range(tiles)], axis=1)
            shares[k][...] = dot_nn(pre, up).astype(bf16)
            value = jnp.concatenate([active_kept[k][j] for j in range(tiles)], axis=1)
            lasts[k][...] = dot_nn(value, down).astype(bf16)


def units(seconds, grads, weights, piece, shift):
    count = len(seconds)
    rows, model = seconds[0].shape
    hidden = weights.shape[0]
    width = min(256, hidden)
    tiles = hidden // width
    turns = model // (2 * piece)
    tile = pl.BlockSpec((rows, width), lambda j: (0, jnp.minimum(j, tiles - 1)))
    whole = pl.BlockSpec((rows, model), lambda j: (0, 0))
    part = pl.BlockSpec((rows, 2 * piece), lambda j: (0, jnp.maximum(j - tiles, 0)))
    out = pl.pallas_call(
        functools.partial(units_kernel, count, piece, tiles),
        grid=(tiles + turns,),
        in_specs=[whole] * (2 * count)
        + [
            pl.BlockSpec((width, 2 * model), lambda j: (jnp.minimum(j, tiles - 1), 0)),
            pl.BlockSpec((hidden, 4 * piece), lambda j: (0, jnp.maximum(j - tiles, 0))),
            pl.BlockSpec((1, width), lambda j: (0, jnp.minimum(j, tiles - 1))),
        ],
        out_specs=[tile] * (2 * count) + [part] * (2 * count),
        out_shape=[jax.ShapeDtypeStruct((rows, hidden), bf16)] * (2 * count)
        + [jax.ShapeDtypeStruct((rows, model), bf16)] * (2 * count),
        scratch_shapes=[pltpu.VMEM((tiles, rows, width), bf16)] * (2 * count),
        cost_estimate=pl.CostEstimate(
            flops=8 * count * rows * model * hidden,
            transcendentals=count * rows * hidden,
            bytes_accessed=8 * hidden * model + 4 * count * rows * (2 * model + hidden),
        ),
        name="units",
    )(*seconds, *grads, weights, weights, shift.reshape(1, hidden))
    return [out[k * count : (k + 1) * count] for k in range(4)]


def rows_product_kernel(depth, owner_ref, left_ref, shift_ref, *refs):
    blocks, out_ref = refs[:-1], refs[-1]
    total = jnp.broadcast_to(shift_ref[...], out_ref.shape)
    for k, block in enumerate(blocks):
        at = pl.multiple_of(owner_ref[k] * depth, depth)
        total = total + dot_nn(left_ref[:, pl.ds(at, depth)], block[...])
    out_ref[...] = total.astype(out_ref.dtype)


def rows_product(left, blocks, owners, shift):
    depth, width = blocks[0].shape
    tile = 128 * max(t for t in range(1, 9) if width % (128 * t) == 0)
    return pl.pallas_call(
        functools.partial(rows_product_kernel, depth),
        grid_spec=pltpu.PrefetchScalarGridSpec(
            num_scalar_prefetch=1,
            grid=(width // tile,),
            in_specs=[
                pl.BlockSpec(left.shape, lambda j, owner: (0, 0)),
                pl.BlockSpec((1, tile), lambda j, owner: (0, j)),
            ]
            + [pl.BlockSpec((depth, tile), lambda j, owner: (0, j)) for _ in blocks],
            out_specs=pl.BlockSpec((left.shape[0], tile), lambda j, owner: (0, j)),
        ),
        out_shape=jax.ShapeDtypeStruct((left.shape[0], width), bf16),
        cost_estimate=pl.CostEstimate(
            flops=2 * left.shape[0] * left.shape[1] * width,
            transcendentals=0,
            bytes_accessed=2 * left.shape[1] * width,
        ),
        name="rows_product",
    )(owners, left, shift.reshape(1, width), *blocks)


def grads_product_kernel(count, *refs):
    out_ref, sum_ref = refs[2 * count :]
    total = dot_tn(refs[0][...], refs[count][...])
    for k in range(1, count):
        total = total + dot_tn(refs[k][...], refs[count + k][...])
    out_ref[...] = total.astype(out_ref.dtype)

    @pl.when(pl.program_id(0) == 0)
    def _():
        sums = jnp.zeros(sum_ref.shape, f32)
        for k in range(count):
            sums = sums + jnp.sum(refs[k][...].astype(f32), axis=0, keepdims=True)
        sum_ref[...] = sums


def grads_product(lefts, rights):
    rows, units = lefts[0].shape
    width = rights[0].shape[1]
    tile = min(512, width)
    count = len(lefts)
    return pl.pallas_call(
        functools.partial(grads_product_kernel, count),
        grid=(width // tile,),
        in_specs=[pl.BlockSpec((rows, units), lambda j: (0, 0)) for _ in lefts]
        + [pl.BlockSpec((rows, tile), lambda j: (0, j)) for _ in rights],
        out_specs=[
            pl.BlockSpec((units, tile), lambda j: (0, j)),
            pl.BlockSpec((1, units), lambda j: (0, 0)),
        ],
        out_shape=[
            jax.ShapeDtypeStruct((units, width), bf16),
            jax.ShapeDtypeStruct((1, units), f32),
        ],
        cost_estimate=pl.CostEstimate(
            flops=2 * count * rows * units * width,
            transcendentals=0,
            bytes_accessed=2 * count * rows * (units + width) + 2 * units * width,
        ),
        name="grads_product",
    )(*lefts, *rights)


def cols_product_kernel(depth, owner_ref, left_ref, *refs):
    blocks, out_ref = refs[:-1], refs[-1]
    left = left_ref[...]
    for k, block in enumerate(blocks):
        at = pl.multiple_of(owner_ref[k] * depth, depth)
        out_ref[:, pl.ds(at, depth)] = dot_nt(left, block[...])


def cols_product(left, blocks, owners):
    depth, width = blocks[0].shape
    rows = left.shape[0]
    out_width = depth * len(blocks)
    return pl.pallas_call(
        functools.partial(cols_product_kernel, depth),
        grid_spec=pltpu.PrefetchScalarGridSpec(
            num_scalar_prefetch=1,
            grid=(left.shape[0] // rows,),
            in_specs=[pl.BlockSpec((rows, width), lambda i, owner: (i, 0))]
            + [pl.BlockSpec((depth, width), lambda i, owner: (0, 0)) for _ in blocks],
            out_specs=pl.BlockSpec((rows, out_width), lambda i, owner: (i, 0)),
        ),
        out_shape=jax.ShapeDtypeStruct((left.shape[0], out_width), f32),
        cost_estimate=pl.CostEstimate(
            flops=2 * left.shape[0] * out_width * width,
            transcendentals=0,
            bytes_accessed=2 * out_width * width,
        ),
        name="cols_product",
    )(owners, left, *blocks)


def on_device(
    tokens,
    segment_ids,
    attngain,
    attnshift,
    queryweight,
    querybias,
    keyvalue,
    valuebias,
    outweight,
    outbias,
    mlpgain,
    mlpshift,
    upweight,
    upbias,
    downweight,
    downbias,
    cotangent,
):
    head_dim = valuebias.shape[0]
    count, model = tokens.shape
    n_dp = lax.axis_size("dp")
    n_tensor = lax.axis_size("tensor")
    dp_index = lax.axis_index("dp")
    tensor_index = lax.axis_index("tensor")
    ring = Ring(n_dp)
    order = ring.keys
    owners = jnp.stack([ring.owner(dp_index, *key) for key in order]).astype(jnp.int32)
    segment = segment_ids[0]
    length = segment.shape[0]
    rows = tokens.astype(f32)
    depth = queryweight.shape[0]
    width = queryweight.shape[1]

    both = lax.all_gather(jnp.stack([queryweight, outweight.T]), "tensor", axis=0)
    both = both.transpose(1, 2, 0, 3).reshape(2, depth, n_tensor * width)

    hidden_own = upweight.shape[1] // n_dp
    bias_part = lax.dynamic_slice_in_dim(upbias, dp_index * hidden_own, hidden_own)
    biases = axis_gather(jnp.concatenate([querybias, bias_part]), "tensor")
    query_shift = biases[:, :width].reshape(-1)
    up_shift = biases[:, width:].reshape(-1)
    pair_full = axis_gather(after(keyvalue, biases), "dp").reshape(model, 2 * head_dim)

    first_mean, first_scale = norm_stats(rows)
    normed_first = ((rows - first_mean) * first_scale * attngain + attnshift).astype(bf16)
    pair_shift = jnp.concatenate([jnp.zeros((head_dim,), f32), valuebias])
    pairs = (dot_nn(normed_first, pair_full) + pair_shift).astype(bf16)

    weights = after(jnp.concatenate([upweight.T, downweight], axis=1), pair_full)
    weights = lax.all_to_all(weights, "dp", 0, 1, tiled=True)
    kv_all = axis_gather(after(pairs, weights), "tensor").reshape(length, 2 * head_dim)

    first_blocks = ring.gather(both[0], (None, None, weights, kv_all))
    first_list = [first_blocks[key] for key in order]
    weights = lax.all_gather(after(weights, kv_all), "tensor", axis=0, tiled=True)

    grads = {(0, 0): cotangent, (1, 0): ring.step(cotangent)}
    normed_late = after(normed_first, grads[(1, 0)])
    queries = rows_product(normed_late, first_list, owners, query_shift)
    if ring.chips > 2:
        grads[(2, 0)] = ring.step(after(grads[(1, 0)], queries))
    keys = 256 if length % 256 == 0 else 128
    query_block = min(128, count)
    first_row = tensor_index * count
    own_segment = lax.dynamic_slice_in_dim(segment, first_row, count)
    starts = jnp.sum(
        (segment[None, :] < own_segment[:, None]).astype(jnp.int32), axis=1
    )
    block_first = first_row + jnp.arange(count // query_block, dtype=jnp.int32) * query_block
    info = jnp.stack(
        [
            starts[::query_block] // keys,
            (block_first + query_block - 1) // keys + 1,
            block_first,
        ]
    ).astype(jnp.int32)
    starts = starts.reshape(1, count)
    mixed, totals = attend_forward(queries, kv_all, info, starts, head_dim, keys)
    for at in range(3, ring.chips):
        grads[(at, 0)] = ring.step(after(grads[(at - 1, 0)], mixed))
    for at in range(ring.chips):
        grads[(at, 1)] = ring.swap(after(grads[(at, 0)], mixed))
    out_blocks = ring.gather(both[1], (None, first_list, queries, mixed))
    out_list = [out_blocks[key] for key in order]
    residual = rows + cols_product(after(mixed, grads[(min(2, ring.chips - 1), 0)]), out_list, owners) + outbias
    second_mean, second_scale = norm_stats(residual)
    normed_second = ((residual - second_mean) * second_scale * mlpgain + mlpshift).astype(bf16)

    active, grad_pre, second_parts, last_parts, seconds = {}, {}, {}, {}, {}
    done = []

    def work(s):
        keys_here = [(s, 0), (s, 1)]
        seconds[keys_here[0]] = passed[s]
        seconds[keys_here[1]] = ring.swap(after(passed[s], done))
        found = units(
            [after(seconds[key], done[-1:]) for key in keys_here],
            [grads[key] for key in keys_here],
            weights,
            depth,
            up_shift,
        )
        done.append(found[2])
        for kept, values in zip((active, grad_pre, second_parts, last_parts), found):
            kept.update(zip(keys_here, values))

    passed = [normed_second]
    for s in range(1, ring.chips):
        if s >= 3:
            work(s - 2)
        passed.append(ring.step(after(passed[-1], done)))
    for s in range(max(1, ring.chips - 2), ring.chips):
        work(s)
    work(0)
    sums = started(ring.sums(second_parts))
    for at in range(ring.chips):
        grad_second = sums.send(done[min(at + 1, len(done) - 1)])
    parts_done = done[-1]
    up_local, upbias_part = grads_product(
        [after(grad_pre[key], parts_done) for key in order], [seconds[key] for key in order]
    )
    up_part = lax.psum_scatter(up_local, "tensor", scatter_dimension=0, tiled=True)
    grad_second = [after(share, up_local) for share in grad_second]
    grad_second += [jnp.zeros_like(cotangent)] * (3 - len(grad_second))

    grad_resid, grad_branch, second_sums = norm_backward_shares(
        grad_second, residual, cotangent, mlpgain
    )
    grad_mixed = rows_product(grad_branch, out_list, owners, jnp.zeros((model,), f32))
    grad_queries, grad_kv = attend_backward(
        queries, grad_mixed, mixed, kv_all, info, starts, totals, head_dim, keys
    )

    def depth_sums(local):
        return started(
            ring.sums(
                {
                    key: lax.dynamic_slice_in_dim(local, owners[k] * depth, depth, 0)
                    for k, key in enumerate(order)
                }
            )
        )

    def width_owner(block):
        parts = block.astype(bf16).reshape(depth, n_tensor, width).transpose(1, 0, 2)
        return lax.psum_scatter(parts, "tensor", scatter_dimension=0, tiled=False).astype(f32)

    chips = ring.chips
    last_sums = started(ring.sums(last_parts))
    last_sent = [last_sums.send(gate) for gate in (grad_mixed, grad_queries)[:chips]]
    pair_raw = tensor_exchange(grad_kv.astype(bf16), count)
    down_local, _ = grads_product(
        [after(active[key], grad_queries, last_sent) for key in order],
        [grads[key] for key in order],
    )
    down_part = lax.psum_scatter(down_local, "tensor", scatter_dimension=0, tiled=True)
    out_local = dot_tn(after(grad_branch, down_local), mixed).astype(bf16)
    out_sums = depth_sums(out_local)
    out_sent = [out_sums.send(None)]
    if chips > 2:
        last_sent.append(last_sums.send(down_local))
    pair_shares = after(pair_raw, down_local)
    grad_pairs = jnp.sum(pair_shares.astype(f32), axis=0).astype(bf16)
    grad_qkv = jnp.concatenate([grad_queries, grad_pairs], axis=1)
    first_local = dot_tn(normed_first, grad_qkv).astype(bf16)
    first_sums = depth_sums(first_local)
    first_sent = [first_sums.send(None) for _ in range(chips)]
    first_part = total(first_sent[-1])
    for at in range(1, chips):
        out_sent.append(out_sums.send(first_part))
    out_part = total(out_sent[-1])
    for at in range(len(last_sent), chips):
        last_sent.append(last_sums.send(first_part))
    layer_out = residual + total(last_sent[-1]) + downbias
    up_grad = lax.all_to_all(after(up_part, first_part), "dp", 1, 0, tiled=True).astype(f32).T
    grad_first = cols_product(after(grad_queries, first_sent[min(1, chips - 1)]), first_list, owners)
    grad_first = grad_first + dot_nt(grad_pairs, pair_full)
    grad_one, attngain_part, attnshift_part = norm_backward(
        rows, first_mean, first_scale, attngain, grad_first
    )
    tokens_grad = (grad_resid + grad_one).astype(bf16)

    shift_part = jnp.sum(grad_qkv.astype(f32), axis=0)
    vectors = [
        attngain_part,
        attnshift_part,
        second_sums[0],
        second_sums[1],
        second_sums[2],
        second_sums[3],
        shift_part[:model],
        shift_part[model + head_dim :],
    ]
    sizes = [v.shape[0] for v in vectors]
    plain = sum(sizes)
    flat = jnp.concatenate(vectors + [upbias_part[0]])
    flat = axis_gather(flat, "dp")
    units_flat = flat[:, plain:].reshape(n_dp, n_tensor, hidden_own)
    units_flat = units_flat.transpose(1, 0, 2).reshape(n_tensor, n_dp * hidden_own)
    flat = jnp.broadcast_to(jnp.sum(flat[:, :plain], axis=0), (n_tensor, plain))
    flat = jnp.concatenate([flat, units_flat], axis=1)

    first_sent = first_part.astype(bf16)
    first_sent = jnp.concatenate(
        [
            first_sent[:, :model].reshape(depth, n_tensor, width).transpose(1, 0, 2),
            jnp.broadcast_to(first_sent[None, :, model:], (n_tensor, depth, 2 * head_dim)),
        ],
        axis=2,
    )
    first_sent = tensor_swaps(first_sent)
    down_grad = lax.all_to_all(after(down_part, up_grad), "dp", 1, 0, tiled=True).astype(f32)
    out_grad = width_owner(after(out_part, first_sent)).T
    flat = lax.all_to_all(after(flat, down_grad), "tensor", 0, 0, tiled=True)
    flat = jnp.sum(flat, axis=0)
    first_grad = jnp.sum(first_sent.astype(f32), axis=0)
    query_grad = first_grad[:, :width]
    keyvalue_grad = first_grad[:, width:]

    upbias_grad = flat[plain : plain + n_dp * hidden_own]
    found = []
    at = 0
    for size in sizes:
        found.append(flat[at : at + size])
        at += size
    attngain_grad, attnshift_grad, mlpgain_grad, mlpshift_grad = found[:4]
    outbias_grad, downbias_grad, query_shift_grad, valuebias_grad = found[4:]
    querybias_grad = lax.dynamic_slice_in_dim(query_shift_grad, tensor_index * width, width)
    return (
        layer_out.astype(bf16),
        tokens_grad,
        attngain_grad,
        attnshift_grad,
        query_grad,
        querybias_grad,
        keyvalue_grad,
        valuebias_grad,
        out_grad,
        outbias_grad,
        mlpgain_grad,
        mlpshift_grad,
        up_grad,
        upbias_grad,
        down_grad,
        downbias_grad,
    )


def solution(mesh):
    return jax.shard_map(
        on_device,
        mesh=mesh,
        in_specs=(
            P(("dp", "tensor"), None),
            P("dp", None),
            P(),
            P(),
            P("dp", "tensor"),
            P("tensor"),
            P("dp", None),
            P(),
            P("tensor", "dp"),
            P(),
            P(),
            P(),
            P("dp", "tensor"),
            P("tensor"),
            P("tensor", "dp"),
            P(),
            P(("dp", "tensor"), None),
        ),
        out_specs=(
            P(("dp", "tensor"), None),
            P(("dp", "tensor"), None),
            P(),
            P(),
            P("dp", "tensor"),
            P("tensor"),
            P("dp", None),
            P(),
            P("tensor", "dp"),
            P(),
            P(),
            P(),
            P("dp", "tensor"),
            P("tensor"),
            P("tensor", "dp"),
            P(),
        ),
        check_vma=False,
    )
```

```python
import functools

import jax
import jax.numpy as jnp
from jax import lax
from jax.experimental import pallas as pl
from jax.experimental.pallas import tpu as pltpu
from jax.sharding import PartitionSpec as P

eps_norm = 1e-05
masked_score = -1e30
log2_e = 1.4426950408889634
bf16 = jnp.bfloat16
f32 = jnp.float32


def dot_nn(left_side, right_side):
    return jnp.dot(left_side, right_side, preferred_element_type=f32)


def dot_tn(left_side, right_side):
    return lax.dot_general(
        left_side, right_side, (((0,), (0,)), ((), ())), preferred_element_type=f32
    )


def dot_nt(left_side, right_side):
    return lax.dot_general(
        left_side, right_side, (((1,), (1,)), ((), ())), preferred_element_type=f32
    )


def norm_stats(values):
    row_mean = jnp.mean(values, axis=-1, keepdims=True)
    centered = values - row_mean
    row_var = jnp.mean(centered * centered, axis=-1, keepdims=True)
    scale = lax.rsqrt(row_var + eps_norm)
    return row_mean, scale


def norm_backward(values, row_mean, scale, gain, grad):
    xhat = (values - row_mean) * scale
    u = grad * gain
    u_mean = jnp.mean(u, axis=-1, keepdims=True)
    ux_mean = jnp.mean(u * xhat, axis=-1, keepdims=True)
    grad_in = (u - u_mean - xhat * ux_mean) * scale
    return grad_in, jnp.sum(grad * xhat, axis=0), jnp.sum(grad, axis=0)


def norm_backward_kernel(
    one_ref, two_ref, three_ref, values_ref, out_ref, gain_ref, resid_ref, branch_ref, sums_ref
):
    grad = one_ref[...].astype(f32) + two_ref[...].astype(f32) + three_ref[...].astype(f32)
    values = values_ref[...]
    grad_out = out_ref[...].astype(f32)
    mean, scale = norm_stats(values)
    xhat = (values - mean) * scale
    u = grad * gain_ref[...]
    u_mean = jnp.mean(u, axis=-1, keepdims=True)
    ux_mean = jnp.mean(u * xhat, axis=-1, keepdims=True)
    resid = grad_out + (u - u_mean - xhat * ux_mean) * scale
    branch = resid.astype(bf16)
    resid_ref[...] = resid
    branch_ref[...] = branch

    @pl.when(pl.program_id(0) == 0)
    def _():
        sums_ref[...] = jnp.zeros_like(sums_ref)

    for k, rows in enumerate((grad * xhat, grad, branch.astype(f32), grad_out)):
        sums_ref[k : k + 1] += jnp.sum(rows, axis=0, keepdims=True)


def norm_backward_shares(shares, values, grad_out, gain):
    count, model = values.shape
    rows = min(128, count)
    tile = pl.BlockSpec((rows, model), lambda i: (i, 0))
    return pl.pallas_call(
        norm_backward_kernel,
        grid=(count // rows,),
        in_specs=[tile] * 5 + [pl.BlockSpec((1, model), lambda i: (0, 0))],
        out_specs=[tile, tile, pl.BlockSpec((8, model), lambda i: (0, 0))],
        out_shape=[
            jax.ShapeDtypeStruct((count, model), f32),
            jax.ShapeDtypeStruct((count, model), bf16),
            jax.ShapeDtypeStruct((8, model), f32),
        ],
        name="norm_backward",
    )(*shares, values, grad_out, gain.reshape(1, model))


gelu_c = 0.7978845608028654


def gelu_both(v):
    square = v * v
    inner = gelu_c * v * (1.0 + 0.044715 * square)
    t = jnp.tanh(inner)
    half = 0.5 * (1.0 + t)
    value = v * half
    slope = half + 0.5 * v * (1.0 - t * t) * (gelu_c * (1.0 + 3.0 * 0.044715 * square))
    return value, slope


def stack_heads(block, heads, width):
    return jnp.concatenate(
        [block[:, h * width : (h + 1) * width] for h in range(heads)], axis=0
    )


def block_bias(first_key, keys, start_row, query_row):
    key_at = first_key + lax.broadcasted_iota(jnp.int32, (keys, start_row.shape[1]), 0)
    allowed = (key_at >= start_row) & (key_at <= query_row)
    return jnp.where(allowed, 0.0, masked_score)


def attend_forward_kernel(
    heads, width, keys, info_ref, q_ref, kv_ref, start_ref, o_ref, total_ref
):
    at = pl.program_id(1)
    rows = q_ref.shape[0]
    q = stack_heads(q_ref[...], heads, width)
    start_row = start_ref[...]
    query_row = info_ref[2, at] + lax.broadcasted_iota(jnp.int32, (1, rows), 1)
    scale = width**-0.5 * log2_e

    def step(block, carried):
        top, total, mixed = carried
        first_key = pl.multiple_of(block * keys, keys)
        k = kv_ref[pl.ds(first_key, keys), :width]
        v = kv_ref[pl.ds(first_key, keys), width:]
        bias = block_bias(first_key, keys, start_row, query_row)
        scores = dot_nt(k, q) * scale + jnp.concatenate([bias] * heads, axis=1)
        new_top = jnp.maximum(top, jnp.max(scores, axis=0, keepdims=True))
        shrink = jnp.exp2(top - new_top)
        part = jnp.exp2(scores - new_top)
        total = total * shrink + jnp.sum(part, axis=0, keepdims=True)
        mixed = mixed * shrink + dot_tn(v, part.astype(bf16))
        return new_top, total, mixed

    count = heads * rows
    top, total, mixed = lax.fori_loop(
        info_ref[0, at],
        info_ref[1, at],
        step,
        (
            jnp.full((1, count), masked_score, f32),
            jnp.zeros((1, count), f32),
            jnp.zeros((width, count), f32),
        ),
    )
    out = (mixed / total).T.astype(bf16)
    for h in range(heads):
        o_ref[:, h * width : (h + 1) * width] = out[h * rows : (h + 1) * rows]
    total_ref[...] = (top + jnp.log2(total)).reshape(total_ref.shape)


def attend_backward_kernel(
    heads,
    width,
    keys,
    info_ref,
    q_ref,
    grad_ref,
    o_ref,
    kv_ref,
    start_ref,
    total_ref,
    dq_ref,
    dkv_ref,
):
    at = pl.program_id(1)
    rows = q_ref.shape[0]

    @pl.when((pl.program_id(0) == 0) & (at == 0))
    def _():
        dkv_ref[...] = jnp.zeros_like(dkv_ref)

    q = stack_heads(q_ref[...], heads, width)
    grad = stack_heads(grad_ref[...], heads, width)
    out = stack_heads(o_ref[...], heads, width)
    delta = jnp.sum((grad.astype(f32) * out.astype(f32)).T, axis=0, keepdims=True)
    count = heads * rows
    total = total_ref[...].reshape(1, count)
    start_row = start_ref[...]
    query_row = info_ref[2, at] + lax.broadcasted_iota(jnp.int32, (1, rows), 1)
    scale = width**-0.5

    def step(block, dq):
        first_key = pl.multiple_of(block * keys, keys)
        k = kv_ref[pl.ds(first_key, keys), :width]
        v = kv_ref[pl.ds(first_key, keys), width:]
        bias = block_bias(first_key, keys, start_row, query_row)
        scores = dot_nt(k, q) * (scale * log2_e) + jnp.concatenate([bias] * heads, axis=1)
        probs = jnp.exp2(scores - total)
        dprobs = dot_nt(v, grad)
        dscores = (probs * (dprobs - delta)).astype(bf16)
        dkv_ref[pl.ds(first_key, keys), :width] += dot_nn(dscores, q) * scale
        dkv_ref[pl.ds(first_key, keys), width:] += dot_nn(probs.astype(bf16), grad)
        return dq + dot_tn(k, dscores)

    dq = lax.fori_loop(
        info_ref[0, at], info_ref[1, at], step, jnp.zeros((width, count), f32)
    )
    dq = (dq * scale).T.astype(bf16)
    for h in range(heads):
        dq_ref[:, h * width : (h + 1) * width] = dq[h * rows : (h + 1) * rows]


def attend_shapes(queries, width):
    tokens = queries.shape[0]
    heads_all = queries.shape[1] // width
    heads = 16 if heads_all % 16 == 0 else heads_all
    rows = min(128, tokens)
    return tokens, heads_all, heads, heads_all // heads, rows, tokens // rows


def attend_forward(queries, kv_all, info, starts, width, keys):
    tokens, heads_all, heads, groups, rows, blocks = attend_shapes(queries, width)
    return pl.pallas_call(
        functools.partial(attend_forward_kernel, heads, width, keys),
        grid_spec=pltpu.PrefetchScalarGridSpec(
            num_scalar_prefetch=1,
            grid=(groups, blocks),
            in_specs=[
                pl.BlockSpec((rows, heads * width), lambda g, i, info: (i, g)),
                pl.BlockSpec(kv_all.shape, lambda g, i, info: (0, 0)),
                pl.BlockSpec((1, rows), lambda g, i, info: (0, i)),
            ],
            out_specs=[
                pl.BlockSpec((rows, heads * width), lambda g, i, info: (i, g)),
                pl.BlockSpec((1, 1, 1, heads * rows), lambda g, i, info: (g, i, 0, 0)),
            ],
        ),
        out_shape=[
            jax.ShapeDtypeStruct((tokens, heads_all * width), bf16),
            jax.ShapeDtypeStruct((groups, blocks, 1, heads * rows), f32),
        ],
        name="attend_forward",
    )(info, queries, kv_all, starts)


def attend_backward(queries, grad, mixed, kv_all, info, starts, totals, width, keys):
    tokens, heads_all, heads, groups, rows, blocks = attend_shapes(queries, width)
    tile = pl.BlockSpec((rows, heads * width), lambda g, i, info: (i, g))
    return pl.pallas_call(
        functools.partial(attend_backward_kernel, heads, width, keys),
        grid_spec=pltpu.PrefetchScalarGridSpec(
            num_scalar_prefetch=1,
            grid=(groups, blocks),
            in_specs=[
                tile,
                tile,
                tile,
                pl.BlockSpec(kv_all.shape, lambda g, i, info: (0, 0)),
                pl.BlockSpec((1, rows), lambda g, i, info: (0, i)),
                pl.BlockSpec((1, 1, 1, heads * rows), lambda g, i, info: (g, i, 0, 0)),
            ],
            out_specs=[
                tile,
                pl.BlockSpec(kv_all.shape, lambda g, i, info: (0, 0)),
            ],
        ),
        out_shape=[
            jax.ShapeDtypeStruct((tokens, heads_all * width), bf16),
            jax.ShapeDtypeStruct(kv_all.shape, f32),
        ],
        name="attend_backward",
    )(info, queries, grad, mixed, kv_all, starts, totals)


def after(value, *earlier):
    return lax.optimization_barrier((value, earlier))[0]


def axis_gather(block, axis):
    copies = jnp.broadcast_to(block[None], (lax.axis_size(axis),) + block.shape)
    return lax.all_to_all(copies, axis, 0, 0)


def tensor_exchange(parts, rows):
    parts = parts.reshape(lax.axis_size("tensor"), rows, parts.shape[1])
    return lax.all_to_all(parts, "tensor", 0, 0)


def tensor_swaps(parts):
    size = lax.axis_size("tensor")
    index = lax.axis_index("tensor")
    found = jnp.zeros(parts.shape, parts.dtype)
    zeros = (0,) * (parts.ndim - 1)
    for s in range(size):
        part = lax.dynamic_index_in_dim(parts, (index + s) % size, 0)
        if s:
            part = lax.ppermute(part, "tensor", [(i, (i + s) % size) for i in range(size)])
        found = lax.dynamic_update_slice(found, part, ((index - s) % size,) + zeros)
    return found


class Ring:
    def __init__(self, size):
        self.size = size
        self.chips = size // 2
        half = self.chips // 2
        if half:
            self.order = list(range(half)) + list(range(self.chips - 1, half - 1, -1))
        else:
            self.order = [0]
        n = self.chips
        self.pairs = []
        for i in range(n):
            here, there = self.order[i], self.order[(i + 1) % n]
            self.pairs += [(2 * here, 2 * there), (2 * there + 1, 2 * here + 1)]
        self.swap_pairs = [(i, i ^ 1) for i in range(size)]
        self.keys = [(s, c) for s in range(n) for c in (0, 1)]

    def owner(self, index, s, c):
        place = [0] * self.chips
        for i, chip in enumerate(self.order):
            place[chip] = i
        at = jnp.array(place, jnp.int32)[index // 2]
        core = index % 2 if c == 0 else 1 - index % 2
        at = (at + jnp.where(core == 0, -s, s)) % self.chips
        return 2 * jnp.array(self.order, jnp.int32)[at] + core

    def step(self, value):
        return lax.ppermute(value, "dp", self.pairs)

    def swap(self, value):
        return lax.ppermute(value, "dp", self.swap_pairs)

    def gather(self, own, gates=()):
        blocks = {(0, 0): own, (0, 1): self.swap(own)}
        for s in range(1, self.chips):
            if s < len(gates) and gates[s] is not None:
                own = after(own, gates[s])
            own = self.step(own)
            blocks[(s, 0)] = own
            blocks[(s, 1)] = self.swap(own)
        return blocks

    def sums(self, parts):
        held = None
        gate = yield
        for s in list(range(1, self.chips)) + [0]:
            there = self.swap(parts[(s, 1)].astype(bf16))
            if gate is not None:
                there = after(there, gate)
            shares = [parts[(s, 0)], there] + ([] if held is None else [held])
            if s:
                value = total(shares).astype(bf16)
                held = self.step(value)
                gate = yield value
            else:
                gate = yield shares


def total(shares):
    return sum(share.astype(f32) for share in shares)


def started(sums):
    next(sums)
    return sums


def units_kernel(count, piece, tiles, *refs):
    seconds, grads = refs[:count], refs[count : 2 * count]
    rows_ref, cols_ref, shift_ref = refs[2 * count : 2 * count + 3]
    outs = refs[2 * count + 3 :]
    actives, pres, shares, lasts = (outs[k * count : (k + 1) * count] for k in range(4))
    active_kept, pre_kept = (outs[k * count : (k + 1) * count] for k in (4, 5))
    at = pl.program_id(0)

    def pieces(block, first):
        width = block.shape[1]
        return jnp.concatenate(
            [block[:, k : k + piece] for k in range(first * piece, width, 2 * piece)], axis=1
        )

    @pl.when(at < tiles)
    def _():
        up, down = pieces(rows_ref, 0), pieces(rows_ref, 1)
        for k in range(count):
            preact = dot_nt(seconds[k][...], up) + shift_ref[...]
            grad_active = dot_nt(grads[k][...], down)
            value, slope = gelu_both(preact)
            value = value.astype(bf16)
            pre = (grad_active * slope).astype(bf16)
            actives[k][...] = value
            pres[k][...] = pre
            active_kept[k][at] = value
            pre_kept[k][at] = pre

    @pl.when(at >= tiles)
    def _():
        up, down = pieces(cols_ref, 0), pieces(cols_ref, 1)
        for k in range(count):
            pre = jnp.concatenate([pre_kept[k][j] for j in range(tiles)], axis=1)
            shares[k][...] = dot_nn(pre, up).astype(bf16)
            value = jnp.concatenate([active_kept[k][j] for j in range(tiles)], axis=1)
            lasts[k][...] = dot_nn(value, down).astype(bf16)


def units(seconds, grads, weights, piece, shift):
    count = len(seconds)
    rows, model = seconds[0].shape
    hidden = weights.shape[0]
    width = min(256, hidden)
    tiles = hidden // width
    turns = model // (2 * piece)
    tile = pl.BlockSpec((rows, width), lambda j: (0, jnp.minimum(j, tiles - 1)))
    whole = pl.BlockSpec((rows, model), lambda j: (0, 0))
    part = pl.BlockSpec((rows, 2 * piece), lambda j: (0, jnp.maximum(j - tiles, 0)))
    out = pl.pallas_call(
        functools.partial(units_kernel, count, piece, tiles),
        grid=(tiles + turns,),
        in_specs=[whole] * (2 * count)
        + [
            pl.BlockSpec((width, 2 * model), lambda j: (jnp.minimum(j, tiles - 1), 0)),
            pl.BlockSpec((hidden, 4 * piece), lambda j: (0, jnp.maximum(j - tiles, 0))),
            pl.BlockSpec((1, width), lambda j: (0, jnp.minimum(j, tiles - 1))),
        ],
        out_specs=[tile] * (2 * count) + [part] * (2 * count),
        out_shape=[jax.ShapeDtypeStruct((rows, hidden), bf16)] * (2 * count)
        + [jax.ShapeDtypeStruct((rows, model), bf16)] * (2 * count),
        scratch_shapes=[pltpu.VMEM((tiles, rows, width), bf16)] * (2 * count),
        cost_estimate=pl.CostEstimate(
            flops=8 * count * rows * model * hidden,
            transcendentals=count * rows * hidden,
            bytes_accessed=8 * hidden * model + 4 * count * rows * (2 * model + hidden),
        ),
        name="units",
    )(*seconds, *grads, weights, weights, shift.reshape(1, hidden))
    return [out[k * count : (k + 1) * count] for k in range(4)]


def rows_product_kernel(depth, owner_ref, left_ref, shift_ref, *refs):
    blocks, out_ref = refs[:-1], refs[-1]
    total = jnp.broadcast_to(shift_ref[...], out_ref.shape)
    for k, block in enumerate(blocks):
        at = pl.multiple_of(owner_ref[k] * depth, depth)
        total = total + dot_nn(left_ref[:, pl.ds(at, depth)], block[...])
    out_ref[...] = total.astype(out_ref.dtype)


def rows_product(left, blocks, owners, shift):
    depth, width = blocks[0].shape
    tile = 128 * max(t for t in range(1, 9) if width % (128 * t) == 0)
    return pl.pallas_call(
        functools.partial(rows_product_kernel, depth),
        grid_spec=pltpu.PrefetchScalarGridSpec(
            num_scalar_prefetch=1,
            grid=(width // tile,),
            in_specs=[
                pl.BlockSpec(left.shape, lambda j, owner: (0, 0)),
                pl.BlockSpec((1, tile), lambda j, owner: (0, j)),
            ]
            + [pl.BlockSpec((depth, tile), lambda j, owner: (0, j)) for _ in blocks],
            out_specs=pl.BlockSpec((left.shape[0], tile), lambda j, owner: (0, j)),
        ),
        out_shape=jax.ShapeDtypeStruct((left.shape[0], width), bf16),
        cost_estimate=pl.CostEstimate(
            flops=2 * left.shape[0] * left.shape[1] * width,
            transcendentals=0,
            bytes_accessed=2 * left.shape[1] * width,
        ),
        name="rows_product",
    )(owners, left, shift.reshape(1, width), *blocks)


def grads_product_kernel(count, *refs):
    out_ref, sum_ref = refs[2 * count :]
    total = dot_tn(refs[0][...], refs[count][...])
    for k in range(1, count):
        total = total + dot_tn(refs[k][...], refs[count + k][...])
    out_ref[...] = total.astype(out_ref.dtype)

    @pl.when(pl.program_id(0) == 0)
    def _():
        sums = jnp.zeros(sum_ref.shape, f32)
        for k in range(count):
            sums = sums + jnp.sum(refs[k][...].astype(f32), axis=0, keepdims=True)
        sum_ref[...] = sums


def grads_product(lefts, rights):
    rows, units = lefts[0].shape
    width = rights[0].shape[1]
    tile = min(512, width)
    count = len(lefts)
    return pl.pallas_call(
        functools.partial(grads_product_kernel, count),
        grid=(width // tile,),
        in_specs=[pl.BlockSpec((rows, units), lambda j: (0, 0)) for _ in lefts]
        + [pl.BlockSpec((rows, tile), lambda j: (0, j)) for _ in rights],
        out_specs=[
            pl.BlockSpec((units, tile), lambda j: (0, j)),
            pl.BlockSpec((1, units), lambda j: (0, 0)),
        ],
        out_shape=[
            jax.ShapeDtypeStruct((units, width), bf16),
            jax.ShapeDtypeStruct((1, units), f32),
        ],
        cost_estimate=pl.CostEstimate(
            flops=2 * count * rows * units * width,
            transcendentals=0,
            bytes_accessed=2 * count * rows * (units + width) + 2 * units * width,
        ),
        name="grads_product",
    )(*lefts, *rights)


def cols_product_kernel(depth, owner_ref, left_ref, *refs):
    blocks, out_ref = refs[:-1], refs[-1]
    left = left_ref[...]
    for k, block in enumerate(blocks):
        at = pl.multiple_of(owner_ref[k] * depth, depth)
        out_ref[:, pl.ds(at, depth)] = dot_nt(left, block[...])


def cols_product(left, blocks, owners):
    depth, width = blocks[0].shape
    rows = left.shape[0]
    out_width = depth * len(blocks)
    return pl.pallas_call(
        functools.partial(cols_product_kernel, depth),
        grid_spec=pltpu.PrefetchScalarGridSpec(
            num_scalar_prefetch=1,
            grid=(left.shape[0] // rows,),
            in_specs=[pl.BlockSpec((rows, width), lambda i, owner: (i, 0))]
            + [pl.BlockSpec((depth, width), lambda i, owner: (0, 0)) for _ in blocks],
            out_specs=pl.BlockSpec((rows, out_width), lambda i, owner: (i, 0)),
        ),
        out_shape=jax.ShapeDtypeStruct((left.shape[0], out_width), f32),
        cost_estimate=pl.CostEstimate(
            flops=2 * left.shape[0] * out_width * width,
            transcendentals=0,
            bytes_accessed=2 * out_width * width,
        ),
        name="cols_product",
    )(owners, left, *blocks)


def on_device(
    tokens,
    segment_ids,
    attngain,
    attnshift,
    queryweight,
    querybias,
    keyvalue,
    valuebias,
    outweight,
    outbias,
    mlpgain,
    mlpshift,
    upweight,
    upbias,
    downweight,
    downbias,
    cotangent,
):
    head_dim = valuebias.shape[0]
    count, model = tokens.shape
    n_dp = lax.axis_size("dp")
    n_tensor = lax.axis_size("tensor")
    dp_index = lax.axis_index("dp")
    tensor_index = lax.axis_index("tensor")
    ring = Ring(n_dp)
    order = ring.keys
    owners = jnp.stack([ring.owner(dp_index, *key) for key in order]).astype(jnp.int32)
    segment = segment_ids[0]
    length = segment.shape[0]
    rows = tokens.astype(f32)
    depth = queryweight.shape[0]
    width = queryweight.shape[1]

    both = lax.all_gather(jnp.stack([queryweight, outweight.T]), "tensor", axis=0)
    both = both.transpose(1, 2, 0, 3).reshape(2, depth, n_tensor * width)

    hidden_own = upweight.shape[1] // n_dp
    bias_part = lax.dynamic_slice_in_dim(upbias, dp_index * hidden_own, hidden_own)
    biases = axis_gather(jnp.concatenate([querybias, bias_part]), "tensor")
    query_shift = biases[:, :width].reshape(-1)
    up_shift = biases[:, width:].reshape(-1)
    pair_full = axis_gather(after(keyvalue, biases), "dp").reshape(model, 2 * head_dim)

    first_mean, first_scale = norm_stats(rows)
    normed_first = ((rows - first_mean) * first_scale * attngain + attnshift).astype(bf16)
    pair_shift = jnp.concatenate([jnp.zeros((head_dim,), f32), valuebias])
    pairs = (dot_nn(normed_first, pair_full) + pair_shift).astype(bf16)

    weights = after(jnp.concatenate([upweight.T, downweight], axis=1), pair_full)
    weights = lax.all_to_all(weights, "dp", 0, 1, tiled=True)
    kv_all = axis_gather(after(pairs, weights), "tensor").reshape(length, 2 * head_dim)

    first_blocks = ring.gather(both[0], (None, None, weights, kv_all))
    first_list = [first_blocks[key] for key in order]
    weights = lax.all_gather(after(weights, kv_all), "tensor", axis=0, tiled=True)

    grads = {(0, 0): cotangent, (1, 0): ring.step(cotangent)}
    normed_late = after(normed_first, grads[(1, 0)])
    queries = rows_product(normed_late, first_list, owners, query_shift)
    if ring.chips > 2:
        grads[(2, 0)] = ring.step(after(grads[(1, 0)], queries))
    keys = 256 if length % 256 == 0 else 128
    query_block = min(128, count)
    first_row = tensor_index * count
    own_segment = lax.dynamic_slice_in_dim(segment, first_row, count)
    starts = jnp.sum(
        (segment[None, :] < own_segment[:, None]).astype(jnp.int32), axis=1
    )
    block_first = first_row + jnp.arange(count // query_block, dtype=jnp.int32) * query_block
    info = jnp.stack(
        [
            starts[::query_block] // keys,
            (block_first + query_block - 1) // keys + 1,
            block_first,
        ]
    ).astype(jnp.int32)
    starts = starts.reshape(1, count)
    mixed, totals = attend_forward(queries, kv_all, info, starts, head_dim, keys)
    for at in range(3, ring.chips):
        grads[(at, 0)] = ring.step(after(grads[(at - 1, 0)], mixed))
    for at in range(ring.chips):
        grads[(at, 1)] = ring.swap(after(grads[(at, 0)], mixed))
    out_blocks = ring.gather(both[1], (None, first_list, queries, mixed))
    out_list = [out_blocks[key] for key in order]
    residual = rows + cols_product(after(mixed, grads[(min(2, ring.chips - 1), 0)]), out_list, owners) + outbias
    second_mean, second_scale = norm_stats(residual)
    normed_second = ((residual - second_mean) * second_scale * mlpgain + mlpshift).astype(bf16)

    active, grad_pre, second_parts, last_parts, seconds = {}, {}, {}, {}, {}
    done = []

    def work(s):
        keys_here = [(s, 0), (s, 1)]
        seconds[keys_here[0]] = passed[s]
        seconds[keys_here[1]] = ring.swap(after(passed[s], done))
        found = units(
            [after(seconds[key], done[-1:]) for key in keys_here],
            [grads[key] for key in keys_here],
            weights,
            depth,
            up_shift,
        )
        done.append(found[2])
        for kept, values in zip((active, grad_pre, second_parts, last_parts), found):
            kept.update(zip(keys_here, values))

    passed = [normed_second]
    for s in range(1, ring.chips):
        if s >= 3:
            work(s - 2)
        passed.append(ring.step(after(passed[-1], done)))
    for s in range(max(1, ring.chips - 2), ring.chips):
        work(s)
    work(0)
    sums = started(ring.sums(second_parts))
    for at in range(ring.chips):
        grad_second = sums.send(done[min(at + 1, len(done) - 1)])
    parts_done = done[-1]
    up_local, upbias_part = grads_product(
        [after(grad_pre[key], parts_done) for key in order], [seconds[key] for key in order]
    )
    up_part = lax.psum_scatter(up_local, "tensor", scatter_dimension=0, tiled=True)
    grad_second = [after(share, up_local) for share in grad_second]
    grad_second += [jnp.zeros_like(cotangent)] * (3 - len(grad_second))

    grad_resid, grad_branch, second_sums = norm_backward_shares(
        grad_second, residual, cotangent, mlpgain
    )
    grad_mixed = rows_product(grad_branch, out_list, owners, jnp.zeros((model,), f32))
    grad_queries, grad_kv = attend_backward(
        queries, grad_mixed, mixed, kv_all, info, starts, totals, head_dim, keys
    )

    def depth_sums(local):
        return started(
            ring.sums(
                {
                    key: lax.dynamic_slice_in_dim(local, owners[k] * depth, depth, 0)
                    for k, key in enumerate(order)
                }
            )
        )

    def width_owner(block):
        parts = block.astype(bf16).reshape(depth, n_tensor, width).transpose(1, 0, 2)
        return lax.psum_scatter(parts, "tensor", scatter_dimension=0, tiled=False).astype(f32)

    chips = ring.chips
    last_sums = started(ring.sums(last_parts))
    last_sent = [last_sums.send(gate) for gate in (grad_mixed, grad_queries)[:chips]]
    pair_raw = tensor_exchange(grad_kv.astype(bf16), count)
    down_local, _ = grads_product(
        [after(active[key], grad_queries, last_sent) for key in order],
        [grads[key] for key in order],
    )
    down_part = lax.psum_scatter(down_local, "tensor", scatter_dimension=0, tiled=True)
    out_local = dot_tn(after(grad_branch, down_local), mixed).astype(bf16)
    out_sums = depth_sums(out_local)
    out_sent = [out_sums.send(None)]
    if chips > 2:
        last_sent.append(last_sums.send(down_local))
    pair_shares = after(pair_raw, down_local)
    grad_pairs = jnp.sum(pair_shares.astype(f32), axis=0).astype(bf16)
    grad_qkv = jnp.concatenate([grad_queries, grad_pairs], axis=1)
    first_local = dot_tn(normed_first, grad_qkv).astype(bf16)
    first_sums = depth_sums(first_local)
    first_sent = [first_sums.send(None) for _ in range(chips)]
    first_part = total(first_sent[-1])
    for at in range(1, chips):
        out_sent.append(out_sums.send(first_part))
    out_part = total(out_sent[-1])
    for at in range(len(last_sent), chips):
        last_sent.append(last_sums.send(first_part))
    layer_out = residual + total(last_sent[-1]) + downbias
    up_grad = lax.all_to_all(after(up_part, first_part), "dp", 1, 0, tiled=True).astype(f32).T
    grad_first = cols_product(after(grad_queries, first_sent[0]), first_list, owners)
    grad_first = grad_first + dot_nt(grad_pairs, pair_full)
    grad_one, attngain_part, attnshift_part = norm_backward(
        rows, first_mean, first_scale, attngain, grad_first
    )
    tokens_grad = (grad_resid + grad_one).astype(bf16)

    shift_part = jnp.sum(grad_qkv.astype(f32), axis=0)
    vectors = [
        attngain_part,
        attnshift_part,
        second_sums[0],
        second_sums[1],
        second_sums[2],
        second_sums[3],
        shift_part[:model],
        shift_part[model + head_dim :],
    ]
    sizes = [v.shape[0] for v in vectors]
    plain = sum(sizes)
    flat = jnp.concatenate(vectors + [upbias_part[0]])
    flat = axis_gather(flat, "dp")
    units_flat = flat[:, plain:].reshape(n_dp, n_tensor, hidden_own)
    units_flat = units_flat.transpose(1, 0, 2).reshape(n_tensor, n_dp * hidden_own)
    flat = jnp.broadcast_to(jnp.sum(flat[:, :plain], axis=0), (n_tensor, plain))
    flat = jnp.concatenate([flat, units_flat], axis=1)

    first_sent = first_part.astype(bf16)
    first_sent = jnp.concatenate(
        [
            first_sent[:, :model].reshape(depth, n_tensor, width).transpose(1, 0, 2),
            jnp.broadcast_to(first_sent[None, :, model:], (n_tensor, depth, 2 * head_dim)),
        ],
        axis=2,
    )
    first_sent = tensor_swaps(first_sent)
    down_grad = lax.all_to_all(after(down_part, up_grad), "dp", 1, 0, tiled=True).astype(f32)
    out_grad = width_owner(after(out_part, first_sent)).T
    flat = lax.all_to_all(after(flat, down_grad), "tensor", 0, 0, tiled=True)
    flat = jnp.sum(flat, axis=0)
    first_grad = jnp.sum(first_sent.astype(f32), axis=0)
    query_grad = first_grad[:, :width]
    keyvalue_grad = first_grad[:, width:]

    upbias_grad = flat[plain : plain + n_dp * hidden_own]
    found = []
    at = 0
    for size in sizes:
        found.append(flat[at : at + size])
        at += size
    attngain_grad, attnshift_grad, mlpgain_grad, mlpshift_grad = found[:4]
    outbias_grad, downbias_grad, query_shift_grad, valuebias_grad = found[4:]
    querybias_grad = lax.dynamic_slice_in_dim(query_shift_grad, tensor_index * width, width)
    return (
        layer_out.astype(bf16),
        tokens_grad,
        attngain_grad,
        attnshift_grad,
        query_grad,
        querybias_grad,
        keyvalue_grad,
        valuebias_grad,
        out_grad,
        outbias_grad,
        mlpgain_grad,
        mlpshift_grad,
        up_grad,
        upbias_grad,
        down_grad,
        downbias_grad,
    )


def solution(mesh):
    return jax.shard_map(
        on_device,
        mesh=mesh,
        in_specs=(
            P(("dp", "tensor"), None),
            P("dp", None),
            P(),
            P(),
            P("dp", "tensor"),
            P("tensor"),
            P("dp", None),
            P(),
            P("tensor", "dp"),
            P(),
            P(),
            P(),
            P("dp", "tensor"),
            P("tensor"),
            P("tensor", "dp"),
            P(),
            P(("dp", "tensor"), None),
        ),
        out_specs=(
            P(("dp", "tensor"), None),
            P(("dp", "tensor"), None),
            P(),
            P(),
            P("dp", "tensor"),
            P("tensor"),
            P("dp", None),
            P(),
            P("tensor", "dp"),
            P(),
            P(),
            P(),
            P("dp", "tensor"),
            P("tensor"),
            P("tensor", "dp"),
            P(),
        ),
        check_vma=False,
    )
```

```python
import functools

import jax
import jax.numpy as jnp
from jax import lax
from jax.experimental import pallas as pl
from jax.experimental.pallas import tpu as pltpu
from jax.sharding import PartitionSpec as P

eps_norm = 1e-05
masked_score = -1e30
log2_e = 1.4426950408889634
bf16 = jnp.bfloat16
f32 = jnp.float32


def dot_nn(left_side, right_side):
    return jnp.dot(left_side, right_side, preferred_element_type=f32)


def dot_tn(left_side, right_side):
    return lax.dot_general(
        left_side, right_side, (((0,), (0,)), ((), ())), preferred_element_type=f32
    )


def dot_nt(left_side, right_side):
    return lax.dot_general(
        left_side, right_side, (((1,), (1,)), ((), ())), preferred_element_type=f32
    )


def norm_stats(values):
    row_mean = jnp.mean(values, axis=-1, keepdims=True)
    centered = values - row_mean
    row_var = jnp.mean(centered * centered, axis=-1, keepdims=True)
    scale = lax.rsqrt(row_var + eps_norm)
    return row_mean, scale


def norm_backward(values, row_mean, scale, gain, grad):
    xhat = (values - row_mean) * scale
    u = grad * gain
    u_mean = jnp.mean(u, axis=-1, keepdims=True)
    ux_mean = jnp.mean(u * xhat, axis=-1, keepdims=True)
    grad_in = (u - u_mean - xhat * ux_mean) * scale
    return grad_in, jnp.sum(grad * xhat, axis=0), jnp.sum(grad, axis=0)


def norm_backward_kernel(
    one_ref, two_ref, three_ref, values_ref, out_ref, gain_ref, resid_ref, branch_ref, sums_ref
):
    grad = one_ref[...].astype(f32) + two_ref[...].astype(f32) + three_ref[...].astype(f32)
    values = values_ref[...]
    grad_out = out_ref[...].astype(f32)
    mean, scale = norm_stats(values)
    xhat = (values - mean) * scale
    u = grad * gain_ref[...]
    u_mean = jnp.mean(u, axis=-1, keepdims=True)
    ux_mean = jnp.mean(u * xhat, axis=-1, keepdims=True)
    resid = grad_out + (u - u_mean - xhat * ux_mean) * scale
    branch = resid.astype(bf16)
    resid_ref[...] = resid
    branch_ref[...] = branch

    @pl.when(pl.program_id(0) == 0)
    def _():
        sums_ref[...] = jnp.zeros_like(sums_ref)

    for k, rows in enumerate((grad * xhat, grad, branch.astype(f32), grad_out)):
        sums_ref[k : k + 1] += jnp.sum(rows, axis=0, keepdims=True)


def norm_backward_shares(shares, values, grad_out, gain):
    count, model = values.shape
    rows = min(128, count)
    tile = pl.BlockSpec((rows, model), lambda i: (i, 0))
    return pl.pallas_call(
        norm_backward_kernel,
        grid=(count // rows,),
        in_specs=[tile] * 5 + [pl.BlockSpec((1, model), lambda i: (0, 0))],
        out_specs=[tile, tile, pl.BlockSpec((8, model), lambda i: (0, 0))],
        out_shape=[
            jax.ShapeDtypeStruct((count, model), f32),
            jax.ShapeDtypeStruct((count, model), bf16),
            jax.ShapeDtypeStruct((8, model), f32),
        ],
        name="norm_backward",
    )(*shares, values, grad_out, gain.reshape(1, model))


gelu_c = 0.7978845608028654


def gelu_both(v):
    square = v * v
    inner = gelu_c * v * (1.0 + 0.044715 * square)
    t = jnp.tanh(inner)
    half = 0.5 * (1.0 + t)
    value = v * half
    slope = half + 0.5 * v * (1.0 - t * t) * (gelu_c * (1.0 + 3.0 * 0.044715 * square))
    return value, slope


def stack_heads(block, heads, width):
    return jnp.concatenate(
        [block[:, h * width : (h + 1) * width] for h in range(heads)], axis=0
    )


def block_bias(first_key, keys, start_row, query_row):
    key_at = first_key + lax.broadcasted_iota(jnp.int32, (keys, start_row.shape[1]), 0)
    allowed = (key_at >= start_row) & (key_at <= query_row)
    return jnp.where(allowed, 0.0, masked_score)


def attend_forward_kernel(
    heads, width, keys, info_ref, q_ref, kv_ref, start_ref, o_ref, total_ref
):
    at = pl.program_id(1)
    rows = q_ref.shape[0]
    q = stack_heads(q_ref[...], heads, width)
    start_row = start_ref[...]
    query_row = info_ref[2, at] + lax.broadcasted_iota(jnp.int32, (1, rows), 1)
    scale = width**-0.5 * log2_e

    def step(block, carried):
        top, total, mixed = carried
        first_key = pl.multiple_of(block * keys, keys)
        k = kv_ref[pl.ds(first_key, keys), :width]
        v = kv_ref[pl.ds(first_key, keys), width:]
        bias = block_bias(first_key, keys, start_row, query_row)
        scores = dot_nt(k, q) * scale + jnp.concatenate([bias] * heads, axis=1)
        new_top = jnp.maximum(top, jnp.max(scores, axis=0, keepdims=True))
        shrink = jnp.exp2(top - new_top)
        part = jnp.exp2(scores - new_top)
        total = total * shrink + jnp.sum(part, axis=0, keepdims=True)
        mixed = mixed * shrink + dot_tn(v, part.astype(bf16))
        return new_top, total, mixed

    count = heads * rows
    top, total, mixed = lax.fori_loop(
        info_ref[0, at],
        info_ref[1, at],
        step,
        (
            jnp.full((1, count), masked_score, f32),
            jnp.zeros((1, count), f32),
            jnp.zeros((width, count), f32),
        ),
    )
    out = (mixed / total).T.astype(bf16)
    for h in range(heads):
        o_ref[:, h * width : (h + 1) * width] = out[h * rows : (h + 1) * rows]
    total_ref[...] = (top + jnp.log2(total)).reshape(total_ref.shape)


def attend_backward_kernel(
    heads,
    width,
    keys,
    info_ref,
    q_ref,
    grad_ref,
    o_ref,
    kv_ref,
    start_ref,
    total_ref,
    dq_ref,
    dkv_ref,
):
    at = pl.program_id(1)
    rows = q_ref.shape[0]

    @pl.when((pl.program_id(0) == 0) & (at == 0))
    def _():
        dkv_ref[...] = jnp.zeros_like(dkv_ref)

    q = stack_heads(q_ref[...], heads, width)
    grad = stack_heads(grad_ref[...], heads, width)
    out = stack_heads(o_ref[...], heads, width)
    delta = jnp.sum((grad.astype(f32) * out.astype(f32)).T, axis=0, keepdims=True)
    count = heads * rows
    total = total_ref[...].reshape(1, count)
    start_row = start_ref[...]
    query_row = info_ref[2, at] + lax.broadcasted_iota(jnp.int32, (1, rows), 1)
    scale = width**-0.5

    def step(block, dq):
        first_key = pl.multiple_of(block * keys, keys)
        k = kv_ref[pl.ds(first_key, keys), :width]
        v = kv_ref[pl.ds(first_key, keys), width:]
        bias = block_bias(first_key, keys, start_row, query_row)
        scores = dot_nt(k, q) * (scale * log2_e) + jnp.concatenate([bias] * heads, axis=1)
        probs = jnp.exp2(scores - total)
        dprobs = dot_nt(v, grad)
        dscores = (probs * (dprobs - delta)).astype(bf16)
        dkv_ref[pl.ds(first_key, keys), :width] += dot_nn(dscores, q) * scale
        dkv_ref[pl.ds(first_key, keys), width:] += dot_nn(probs.astype(bf16), grad)
        return dq + dot_tn(k, dscores)

    dq = lax.fori_loop(
        info_ref[0, at], info_ref[1, at], step, jnp.zeros((width, count), f32)
    )
    dq = (dq * scale).T.astype(bf16)
    for h in range(heads):
        dq_ref[:, h * width : (h + 1) * width] = dq[h * rows : (h + 1) * rows]


def attend_shapes(queries, width):
    tokens = queries.shape[0]
    heads_all = queries.shape[1] // width
    heads = 16 if heads_all % 16 == 0 else heads_all
    rows = min(128, tokens)
    return tokens, heads_all, heads, heads_all // heads, rows, tokens // rows


def attend_forward(queries, kv_all, info, starts, width, keys):
    tokens, heads_all, heads, groups, rows, blocks = attend_shapes(queries, width)
    return pl.pallas_call(
        functools.partial(attend_forward_kernel, heads, width, keys),
        grid_spec=pltpu.PrefetchScalarGridSpec(
            num_scalar_prefetch=1,
            grid=(groups, blocks),
            in_specs=[
                pl.BlockSpec((rows, heads * width), lambda g, i, info: (i, g)),
                pl.BlockSpec(kv_all.shape, lambda g, i, info: (0, 0)),
                pl.BlockSpec((1, rows), lambda g, i, info: (0, i)),
            ],
            out_specs=[
                pl.BlockSpec((rows, heads * width), lambda g, i, info: (i, g)),
                pl.BlockSpec((1, 1, 1, heads * rows), lambda g, i, info: (g, i, 0, 0)),
            ],
        ),
        out_shape=[
            jax.ShapeDtypeStruct((tokens, heads_all * width), bf16),
            jax.ShapeDtypeStruct((groups, blocks, 1, heads * rows), f32),
        ],
        name="attend_forward",
    )(info, queries, kv_all, starts)


def attend_backward(queries, grad, mixed, kv_all, info, starts, totals, width, keys):
    tokens, heads_all, heads, groups, rows, blocks = attend_shapes(queries, width)
    tile = pl.BlockSpec((rows, heads * width), lambda g, i, info: (i, g))
    return pl.pallas_call(
        functools.partial(attend_backward_kernel, heads, width, keys),
        grid_spec=pltpu.PrefetchScalarGridSpec(
            num_scalar_prefetch=1,
            grid=(groups, blocks),
            in_specs=[
                tile,
                tile,
                tile,
                pl.BlockSpec(kv_all.shape, lambda g, i, info: (0, 0)),
                pl.BlockSpec((1, rows), lambda g, i, info: (0, i)),
                pl.BlockSpec((1, 1, 1, heads * rows), lambda g, i, info: (g, i, 0, 0)),
            ],
            out_specs=[
                tile,
                pl.BlockSpec(kv_all.shape, lambda g, i, info: (0, 0)),
            ],
        ),
        out_shape=[
            jax.ShapeDtypeStruct((tokens, heads_all * width), bf16),
            jax.ShapeDtypeStruct(kv_all.shape, f32),
        ],
        name="attend_backward",
    )(info, queries, grad, mixed, kv_all, starts, totals)


def after(value, *earlier):
    return lax.optimization_barrier((value, earlier))[0]


def axis_gather(block, axis):
    copies = jnp.broadcast_to(block[None], (lax.axis_size(axis),) + block.shape)
    return lax.all_to_all(copies, axis, 0, 0)


def tensor_exchange(parts, rows):
    parts = parts.reshape(lax.axis_size("tensor"), rows, parts.shape[1])
    return lax.all_to_all(parts, "tensor", 0, 0)


def tensor_swaps(parts):
    size = lax.axis_size("tensor")
    index = lax.axis_index("tensor")
    found = jnp.zeros(parts.shape, parts.dtype)
    zeros = (0,) * (parts.ndim - 1)
    for s in range(size):
        part = lax.dynamic_index_in_dim(parts, (index + s) % size, 0)
        if s:
            part = lax.ppermute(part, "tensor", [(i, (i + s) % size) for i in range(size)])
        found = lax.dynamic_update_slice(found, part, ((index - s) % size,) + zeros)
    return found


class Ring:
    def __init__(self, size):
        self.size = size
        self.chips = size // 2
        half = self.chips // 2
        if half:
            self.order = list(range(half)) + list(range(self.chips - 1, half - 1, -1))
        else:
            self.order = [0]
        n = self.chips
        self.pairs = []
        for i in range(n):
            here, there = self.order[i], self.order[(i + 1) % n]
            self.pairs += [(2 * here, 2 * there), (2 * there + 1, 2 * here + 1)]
        self.swap_pairs = [(i, i ^ 1) for i in range(size)]
        self.keys = [(s, c) for s in range(n) for c in (0, 1)]

    def owner(self, index, s, c):
        place = [0] * self.chips
        for i, chip in enumerate(self.order):
            place[chip] = i
        at = jnp.array(place, jnp.int32)[index // 2]
        core = index % 2 if c == 0 else 1 - index % 2
        at = (at + jnp.where(core == 0, -s, s)) % self.chips
        return 2 * jnp.array(self.order, jnp.int32)[at] + core

    def step(self, value):
        return lax.ppermute(value, "dp", self.pairs)

    def swap(self, value):
        return lax.ppermute(value, "dp", self.swap_pairs)

    def gather(self, own, gates=()):
        blocks = {(0, 0): own, (0, 1): self.swap(own)}
        for s in range(1, self.chips):
            if s < len(gates) and gates[s] is not None:
                own = after(own, gates[s])
            own = self.step(own)
            blocks[(s, 0)] = own
            blocks[(s, 1)] = self.swap(own)
        return blocks

    def sums(self, parts):
        held = None
        gate = yield
        for s in list(range(1, self.chips)) + [0]:
            there = self.swap(parts[(s, 1)].astype(bf16))
            if gate is not None:
                there = after(there, gate)
            shares = [parts[(s, 0)], there] + ([] if held is None else [held])
            if s:
                value = total(shares).astype(bf16)
                held = self.step(value)
                gate = yield value
            else:
                gate = yield shares


def total(shares):
    return sum(share.astype(f32) for share in shares)


def started(sums):
    next(sums)
    return sums


def units_kernel(count, piece, tiles, *refs):
    seconds, grads = refs[:count], refs[count : 2 * count]
    rows_ref, cols_ref, shift_ref = refs[2 * count : 2 * count + 3]
    outs = refs[2 * count + 3 :]
    actives, pres, shares, lasts = (outs[k * count : (k + 1) * count] for k in range(4))
    active_kept, pre_kept = (outs[k * count : (k + 1) * count] for k in (4, 5))
    at = pl.program_id(0)

    def pieces(block, first):
        width = block.shape[1]
        return jnp.concatenate(
            [block[:, k : k + piece] for k in range(first * piece, width, 2 * piece)], axis=1
        )

    @pl.when(at < tiles)
    def _():
        up, down = pieces(rows_ref, 0), pieces(rows_ref, 1)
        for k in range(count):
            preact = dot_nt(seconds[k][...], up) + shift_ref[...]
            grad_active = dot_nt(grads[k][...], down)
            value, slope = gelu_both(preact)
            value = value.astype(bf16)
            pre = (grad_active * slope).astype(bf16)
            actives[k][...] = value
            pres[k][...] = pre
            active_kept[k][at] = value
            pre_kept[k][at] = pre

    @pl.when(at >= tiles)
    def _():
        up, down = pieces(cols_ref, 0), pieces(cols_ref, 1)
        for k in range(count):
            pre = jnp.concatenate([pre_kept[k][j] for j in range(tiles)], axis=1)
            shares[k][...] = dot_nn(pre, up).astype(bf16)
            value = jnp.concatenate([active_kept[k][j] for j in range(tiles)], axis=1)
            lasts[k][...] = dot_nn(value, down).astype(bf16)


def units(seconds, grads, weights, piece, shift):
    count = len(seconds)
    rows, model = seconds[0].shape
    hidden = weights.shape[0]
    width = min(256, hidden)
    tiles = hidden // width
    turns = model // (2 * piece)
    tile = pl.BlockSpec((rows, width), lambda j: (0, jnp.minimum(j, tiles - 1)))
    whole = pl.BlockSpec((rows, model), lambda j: (0, 0))
    part = pl.BlockSpec((rows, 2 * piece), lambda j: (0, jnp.maximum(j - tiles, 0)))
    out = pl.pallas_call(
        functools.partial(units_kernel, count, piece, tiles),
        grid=(tiles + turns,),
        in_specs=[whole] * (2 * count)
        + [
            pl.BlockSpec((width, 2 * model), lambda j: (jnp.minimum(j, tiles - 1), 0)),
            pl.BlockSpec((hidden, 4 * piece), lambda j: (0, jnp.maximum(j - tiles, 0))),
            pl.BlockSpec((1, width), lambda j: (0, jnp.minimum(j, tiles - 1))),
        ],
        out_specs=[tile] * (2 * count) + [part] * (2 * count),
        out_shape=[jax.ShapeDtypeStruct((rows, hidden), bf16)] * (2 * count)
        + [jax.ShapeDtypeStruct((rows, model), bf16)] * (2 * count),
        scratch_shapes=[pltpu.VMEM((tiles, rows, width), bf16)] * (2 * count),
        cost_estimate=pl.CostEstimate(
            flops=8 * count * rows * model * hidden,
            transcendentals=count * rows * hidden,
            bytes_accessed=8 * hidden * model + 4 * count * rows * (2 * model + hidden),
        ),
        name="units",
    )(*seconds, *grads, weights, weights, shift.reshape(1, hidden))
    return [out[k * count : (k + 1) * count] for k in range(4)]


def rows_product_kernel(depth, owner_ref, left_ref, shift_ref, *refs):
    blocks, out_ref = refs[:-1], refs[-1]
    total = jnp.broadcast_to(shift_ref[...], out_ref.shape)
    for k, block in enumerate(blocks):
        at = pl.multiple_of(owner_ref[k] * depth, depth)
        total = total + dot_nn(left_ref[:, pl.ds(at, depth)], block[...])
    out_ref[...] = total.astype(out_ref.dtype)


def rows_product(left, blocks, owners, shift):
    depth, width = blocks[0].shape
    tile = 128 * max(t for t in range(1, 9) if width % (128 * t) == 0)
    return pl.pallas_call(
        functools.partial(rows_product_kernel, depth),
        grid_spec=pltpu.PrefetchScalarGridSpec(
            num_scalar_prefetch=1,
            grid=(width // tile,),
            in_specs=[
                pl.BlockSpec(left.shape, lambda j, owner: (0, 0)),
                pl.BlockSpec((1, tile), lambda j, owner: (0, j)),
            ]
            + [pl.BlockSpec((depth, tile), lambda j, owner: (0, j)) for _ in blocks],
            out_specs=pl.BlockSpec((left.shape[0], tile), lambda j, owner: (0, j)),
        ),
        out_shape=jax.ShapeDtypeStruct((left.shape[0], width), bf16),
        cost_estimate=pl.CostEstimate(
            flops=2 * left.shape[0] * left.shape[1] * width,
            transcendentals=0,
            bytes_accessed=2 * left.shape[1] * width,
        ),
        name="rows_product",
    )(owners, left, shift.reshape(1, width), *blocks)


def grads_product_kernel(count, *refs):
    out_ref, sum_ref = refs[2 * count :]
    total = dot_tn(refs[0][...], refs[count][...])
    for k in range(1, count):
        total = total + dot_tn(refs[k][...], refs[count + k][...])
    out_ref[...] = total.astype(out_ref.dtype)

    @pl.when(pl.program_id(0) == 0)
    def _():
        sums = jnp.zeros(sum_ref.shape, f32)
        for k in range(count):
            sums = sums + jnp.sum(refs[k][...].astype(f32), axis=0, keepdims=True)
        sum_ref[...] = sums


def grads_product(lefts, rights):
    rows, units = lefts[0].shape
    width = rights[0].shape[1]
    tile = min(512, width)
    count = len(lefts)
    return pl.pallas_call(
        functools.partial(grads_product_kernel, count),
        grid=(width // tile,),
        in_specs=[pl.BlockSpec((rows, units), lambda j: (0, 0)) for _ in lefts]
        + [pl.BlockSpec((rows, tile), lambda j: (0, j)) for _ in rights],
        out_specs=[
            pl.BlockSpec((units, tile), lambda j: (0, j)),
            pl.BlockSpec((1, units), lambda j: (0, 0)),
        ],
        out_shape=[
            jax.ShapeDtypeStruct((units, width), bf16),
            jax.ShapeDtypeStruct((1, units), f32),
        ],
        cost_estimate=pl.CostEstimate(
            flops=2 * count * rows * units * width,
            transcendentals=0,
            bytes_accessed=2 * count * rows * (units + width) + 2 * units * width,
        ),
        name="grads_product",
    )(*lefts, *rights)


def cols_product_kernel(depth, owner_ref, left_ref, *refs):
    blocks, out_ref = refs[:-1], refs[-1]
    left = left_ref[...]
    for k, block in enumerate(blocks):
        at = pl.multiple_of(owner_ref[k] * depth, depth)
        out_ref[:, pl.ds(at, depth)] = dot_nt(left, block[...])


def cols_product(left, blocks, owners):
    depth, width = blocks[0].shape
    rows = left.shape[0]
    out_width = depth * len(blocks)
    return pl.pallas_call(
        functools.partial(cols_product_kernel, depth),
        grid_spec=pltpu.PrefetchScalarGridSpec(
            num_scalar_prefetch=1,
            grid=(left.shape[0] // rows,),
            in_specs=[pl.BlockSpec((rows, width), lambda i, owner: (i, 0))]
            + [pl.BlockSpec((depth, width), lambda i, owner: (0, 0)) for _ in blocks],
            out_specs=pl.BlockSpec((rows, out_width), lambda i, owner: (i, 0)),
        ),
        out_shape=jax.ShapeDtypeStruct((left.shape[0], out_width), f32),
        cost_estimate=pl.CostEstimate(
            flops=2 * left.shape[0] * out_width * width,
            transcendentals=0,
            bytes_accessed=2 * out_width * width,
        ),
        name="cols_product",
    )(owners, left, *blocks)


def on_device(
    tokens,
    segment_ids,
    attngain,
    attnshift,
    queryweight,
    querybias,
    keyvalue,
    valuebias,
    outweight,
    outbias,
    mlpgain,
    mlpshift,
    upweight,
    upbias,
    downweight,
    downbias,
    cotangent,
):
    head_dim = valuebias.shape[0]
    count, model = tokens.shape
    n_dp = lax.axis_size("dp")
    n_tensor = lax.axis_size("tensor")
    dp_index = lax.axis_index("dp")
    tensor_index = lax.axis_index("tensor")
    ring = Ring(n_dp)
    order = ring.keys
    owners = jnp.stack([ring.owner(dp_index, *key) for key in order]).astype(jnp.int32)
    segment = segment_ids[0]
    length = segment.shape[0]
    rows = tokens.astype(f32)
    depth = queryweight.shape[0]
    width = queryweight.shape[1]

    both = lax.all_gather(jnp.stack([queryweight, outweight.T]), "tensor", axis=0)
    both = both.transpose(1, 2, 0, 3).reshape(2, depth, n_tensor * width)

    hidden_own = upweight.shape[1] // n_dp
    bias_part = lax.dynamic_slice_in_dim(upbias, dp_index * hidden_own, hidden_own)
    biases = axis_gather(jnp.concatenate([querybias, bias_part]), "tensor")
    query_shift = biases[:, :width].reshape(-1)
    up_shift = biases[:, width:].reshape(-1)
    pair_full = axis_gather(after(keyvalue, biases), "dp").reshape(model, 2 * head_dim)

    first_mean, first_scale = norm_stats(rows)
    normed_first = ((rows - first_mean) * first_scale * attngain + attnshift).astype(bf16)
    pair_shift = jnp.concatenate([jnp.zeros((head_dim,), f32), valuebias])
    pairs = (dot_nn(normed_first, pair_full) + pair_shift).astype(bf16)

    weights = after(jnp.concatenate([upweight.T, downweight], axis=1), pair_full)
    weights = lax.all_to_all(weights, "dp", 0, 1, tiled=True)
    kv_all = axis_gather(after(pairs, weights), "tensor").reshape(length, 2 * head_dim)

    first_blocks = ring.gather(both[0], (None, None, weights, kv_all))
    first_list = [first_blocks[key] for key in order]
    weights = lax.all_gather(after(weights, kv_all), "tensor", axis=0, tiled=True)

    grads = {(0, 0): cotangent, (1, 0): ring.step(cotangent)}
    normed_late = after(normed_first, grads[(1, 0)])
    queries = rows_product(normed_late, first_list, owners, query_shift)
    if ring.chips > 2:
        grads[(2, 0)] = ring.step(after(grads[(1, 0)], queries))
    keys = 256 if length % 256 == 0 else 128
    query_block = min(128, count)
    first_row = tensor_index * count
    own_segment = lax.dynamic_slice_in_dim(segment, first_row, count)
    starts = jnp.sum(
        (segment[None, :] < own_segment[:, None]).astype(jnp.int32), axis=1
    )
    block_first = first_row + jnp.arange(count // query_block, dtype=jnp.int32) * query_block
    info = jnp.stack(
        [
            starts[::query_block] // keys,
            (block_first + query_block - 1) // keys + 1,
            block_first,
        ]
    ).astype(jnp.int32)
    starts = starts.reshape(1, count)
    mixed, totals = attend_forward(queries, kv_all, info, starts, head_dim, keys)
    for at in range(3, ring.chips):
        grads[(at, 0)] = ring.step(after(grads[(at - 1, 0)], mixed))
    for at in range(ring.chips):
        grads[(at, 1)] = ring.swap(after(grads[(at, 0)], mixed))
    out_blocks = ring.gather(both[1], (None, first_list, queries, mixed))
    out_list = [out_blocks[key] for key in order]
    residual = rows + cols_product(after(mixed, grads[(min(2, ring.chips - 1), 0)]), out_list, owners) + outbias
    second_mean, second_scale = norm_stats(residual)
    normed_second = ((residual - second_mean) * second_scale * mlpgain + mlpshift).astype(bf16)

    active, grad_pre, second_parts, last_parts, seconds = {}, {}, {}, {}, {}
    done = []

    def work(s):
        keys_here = [(s, 0), (s, 1)]
        seconds[keys_here[0]] = passed[s]
        seconds[keys_here[1]] = ring.swap(after(passed[s], done))
        found = units(
            [after(seconds[key], done[-1:]) for key in keys_here],
            [grads[key] for key in keys_here],
            weights,
            depth,
            up_shift,
        )
        done.append(found[2])
        for kept, values in zip((active, grad_pre, second_parts, last_parts), found):
            kept.update(zip(keys_here, values))

    passed = [normed_second]
    for s in range(1, ring.chips):
        if s >= 3:
            work(s - 2)
        passed.append(ring.step(after(passed[-1], done)))
    for s in range(max(1, ring.chips - 2), ring.chips):
        work(s)
    work(0)
    sums = started(ring.sums(second_parts))
    for at in range(ring.chips):
        grad_second = sums.send(done[min(at + 1, len(done) - 1)])
    parts_done = done[-1]
    up_local, upbias_part = grads_product(
        [after(grad_pre[key], parts_done) for key in order], [seconds[key] for key in order]
    )
    up_part = lax.psum_scatter(up_local, "tensor", scatter_dimension=0, tiled=True)
    grad_second = [after(share, up_local) for share in grad_second]
    grad_second += [jnp.zeros_like(cotangent)] * (3 - len(grad_second))

    grad_resid, grad_branch, second_sums = norm_backward_shares(
        grad_second, residual, cotangent, mlpgain
    )
    grad_mixed = rows_product(grad_branch, out_list, owners, jnp.zeros((model,), f32))
    grad_queries, grad_kv = attend_backward(
        queries, grad_mixed, mixed, kv_all, info, starts, totals, head_dim, keys
    )

    def depth_sums(local):
        return started(
            ring.sums(
                {
                    key: lax.dynamic_slice_in_dim(local, owners[k] * depth, depth, 0)
                    for k, key in enumerate(order)
                }
            )
        )

    def width_owner(block):
        parts = block.astype(bf16).reshape(depth, n_tensor, width).transpose(1, 0, 2)
        return lax.psum_scatter(parts, "tensor", scatter_dimension=0, tiled=False).astype(f32)

    chips = ring.chips
    last_sums = started(ring.sums(last_parts))
    last_sent = [last_sums.send(gate) for gate in (grad_mixed, grad_queries)[:chips]]
    pair_raw = tensor_exchange(grad_kv.astype(bf16), count)
    down_local, _ = grads_product(
        [after(active[key], grad_queries, last_sent) for key in order],
        [grads[key] for key in order],
    )
    down_part = lax.psum_scatter(down_local, "tensor", scatter_dimension=0, tiled=True)
    out_local = dot_tn(after(grad_branch, down_local), mixed).astype(bf16)
    out_sums = depth_sums(out_local)
    out_sent = [out_sums.send(None)]
    if chips > 2:
        last_sent.append(last_sums.send(down_local))
    pair_shares = after(pair_raw, down_local)
    grad_pairs = jnp.sum(pair_shares.astype(f32), axis=0).astype(bf16)
    grad_qkv = jnp.concatenate([grad_queries, grad_pairs], axis=1)
    first_local = dot_tn(normed_first, grad_qkv).astype(bf16)
    first_sums = depth_sums(first_local)
    first_sent = [first_sums.send(None) for _ in range(chips - 1)]
    grad_first = cols_product(after(grad_queries, first_sent[min(1, chips - 1)]), first_list, owners)
    grad_first = grad_first + dot_nt(grad_pairs, pair_full)
    grad_one, attngain_part, attnshift_part = norm_backward(
        rows, first_mean, first_scale, attngain, grad_first
    )
    tokens_grad = (grad_resid + grad_one).astype(bf16)

    shift_part = jnp.sum(grad_qkv.astype(f32), axis=0)
    vectors = [
        attngain_part,
        attnshift_part,
        second_sums[0],
        second_sums[1],
        second_sums[2],
        second_sums[3],
        shift_part[:model],
        shift_part[model + head_dim :],
    ]
    sizes = [v.shape[0] for v in vectors]
    plain = sum(sizes)
    flat = jnp.concatenate(vectors + [upbias_part[0]])
    flat = axis_gather(flat, "dp")
    first_sent.append(first_sums.send(flat))
    first_part = total(first_sent[-1])
    for at in range(1, chips):
        out_sent.append(out_sums.send(first_part))
    out_part = total(out_sent[-1])
    for at in range(len(last_sent), chips):
        last_sent.append(last_sums.send(first_part))
    layer_out = residual + total(last_sent[-1]) + downbias
    up_grad = lax.all_to_all(after(up_part, first_part), "dp", 1, 0, tiled=True).astype(f32).T
    units_flat = flat[:, plain:].reshape(n_dp, n_tensor, hidden_own)
    units_flat = units_flat.transpose(1, 0, 2).reshape(n_tensor, n_dp * hidden_own)
    flat = jnp.broadcast_to(jnp.sum(flat[:, :plain], axis=0), (n_tensor, plain))
    flat = jnp.concatenate([flat, units_flat], axis=1)

    first_sent = first_part.astype(bf16)
    first_sent = jnp.concatenate(
        [
            first_sent[:, :model].reshape(depth, n_tensor, width).transpose(1, 0, 2),
            jnp.broadcast_to(first_sent[None, :, model:], (n_tensor, depth, 2 * head_dim)),
        ],
        axis=2,
    )
    first_sent = tensor_swaps(first_sent)
    down_grad = lax.all_to_all(after(down_part, up_grad), "dp", 1, 0, tiled=True).astype(f32)
    out_grad = width_owner(after(out_part, first_sent)).T
    flat = lax.all_to_all(after(flat, down_grad), "tensor", 0, 0, tiled=True)
    flat = jnp.sum(flat, axis=0)
    first_grad = jnp.sum(first_sent.astype(f32), axis=0)
    query_grad = first_grad[:, :width]
    keyvalue_grad = first_grad[:, width:]

    upbias_grad = flat[plain : plain + n_dp * hidden_own]
    found = []
    at = 0
    for size in sizes:
        found.append(flat[at : at + size])
        at += size
    attngain_grad, attnshift_grad, mlpgain_grad, mlpshift_grad = found[:4]
    outbias_grad, downbias_grad, query_shift_grad, valuebias_grad = found[4:]
    querybias_grad = lax.dynamic_slice_in_dim(query_shift_grad, tensor_index * width, width)
    return (
        layer_out.astype(bf16),
        tokens_grad,
        attngain_grad,
        attnshift_grad,
        query_grad,
        querybias_grad,
        keyvalue_grad,
        valuebias_grad,
        out_grad,
        outbias_grad,
        mlpgain_grad,
        mlpshift_grad,
        up_grad,
        upbias_grad,
        down_grad,
        downbias_grad,
    )


def solution(mesh):
    return jax.shard_map(
        on_device,
        mesh=mesh,
        in_specs=(
            P(("dp", "tensor"), None),
            P("dp", None),
            P(),
            P(),
            P("dp", "tensor"),
            P("tensor"),
            P("dp", None),
            P(),
            P("tensor", "dp"),
            P(),
            P(),
            P(),
            P("dp", "tensor"),
            P("tensor"),
            P("tensor", "dp"),
            P(),
            P(("dp", "tensor"), None),
        ),
        out_specs=(
            P(("dp", "tensor"), None),
            P(("dp", "tensor"), None),
            P(),
            P(),
            P("dp", "tensor"),
            P("tensor"),
            P("dp", None),
            P(),
            P("tensor", "dp"),
            P(),
            P(),
            P(),
            P("dp", "tensor"),
            P("tensor"),
            P("tensor", "dp"),
            P(),
        ),
        check_vma=False,
    )
```

```python
import functools

import jax
import jax.numpy as jnp
from jax import lax
from jax.experimental import pallas as pl
from jax.experimental.pallas import tpu as pltpu
from jax.sharding import PartitionSpec as P

eps_norm = 1e-05
masked_score = -1e30
log2_e = 1.4426950408889634
bf16 = jnp.bfloat16
f32 = jnp.float32


def dot_nn(left_side, right_side):
    return jnp.dot(left_side, right_side, preferred_element_type=f32)


def dot_tn(left_side, right_side):
    return lax.dot_general(
        left_side, right_side, (((0,), (0,)), ((), ())), preferred_element_type=f32
    )


def dot_nt(left_side, right_side):
    return lax.dot_general(
        left_side, right_side, (((1,), (1,)), ((), ())), preferred_element_type=f32
    )


def norm_stats(values):
    row_mean = jnp.mean(values, axis=-1, keepdims=True)
    centered = values - row_mean
    row_var = jnp.mean(centered * centered, axis=-1, keepdims=True)
    scale = lax.rsqrt(row_var + eps_norm)
    return row_mean, scale


def norm_backward(values, row_mean, scale, gain, grad):
    xhat = (values - row_mean) * scale
    u = grad * gain
    u_mean = jnp.mean(u, axis=-1, keepdims=True)
    ux_mean = jnp.mean(u * xhat, axis=-1, keepdims=True)
    grad_in = (u - u_mean - xhat * ux_mean) * scale
    return grad_in, jnp.sum(grad * xhat, axis=0), jnp.sum(grad, axis=0)


def norm_backward_kernel(
    one_ref, two_ref, three_ref, values_ref, out_ref, gain_ref, resid_ref, branch_ref, sums_ref
):
    grad = one_ref[...].astype(f32) + two_ref[...].astype(f32) + three_ref[...].astype(f32)
    values = values_ref[...]
    grad_out = out_ref[...].astype(f32)
    mean, scale = norm_stats(values)
    xhat = (values - mean) * scale
    u = grad * gain_ref[...]
    u_mean = jnp.mean(u, axis=-1, keepdims=True)
    ux_mean = jnp.mean(u * xhat, axis=-1, keepdims=True)
    resid = grad_out + (u - u_mean - xhat * ux_mean) * scale
    branch = resid.astype(bf16)
    resid_ref[...] = resid
    branch_ref[...] = branch

    @pl.when(pl.program_id(0) == 0)
    def _():
        sums_ref[...] = jnp.zeros_like(sums_ref)

    for k, rows in enumerate((grad * xhat, grad, branch.astype(f32), grad_out)):
        sums_ref[k : k + 1] += jnp.sum(rows, axis=0, keepdims=True)


def norm_backward_shares(shares, values, grad_out, gain):
    count, model = values.shape
    rows = min(128, count)
    tile = pl.BlockSpec((rows, model), lambda i: (i, 0))
    return pl.pallas_call(
        norm_backward_kernel,
        grid=(count // rows,),
        in_specs=[tile] * 5 + [pl.BlockSpec((1, model), lambda i: (0, 0))],
        out_specs=[tile, tile, pl.BlockSpec((8, model), lambda i: (0, 0))],
        out_shape=[
            jax.ShapeDtypeStruct((count, model), f32),
            jax.ShapeDtypeStruct((count, model), bf16),
            jax.ShapeDtypeStruct((8, model), f32),
        ],
        name="norm_backward",
    )(*shares, values, grad_out, gain.reshape(1, model))


gelu_c = 0.7978845608028654


def gelu_both(v):
    square = v * v
    inner = gelu_c * v * (1.0 + 0.044715 * square)
    t = jnp.tanh(inner)
    half = 0.5 * (1.0 + t)
    value = v * half
    slope = half + 0.5 * v * (1.0 - t * t) * (gelu_c * (1.0 + 3.0 * 0.044715 * square))
    return value, slope


def stack_heads(block, heads, width):
    return jnp.concatenate(
        [block[:, h * width : (h + 1) * width] for h in range(heads)], axis=0
    )


def block_bias(first_key, keys, start_row, query_row):
    key_at = first_key + lax.broadcasted_iota(jnp.int32, (keys, start_row.shape[1]), 0)
    allowed = (key_at >= start_row) & (key_at <= query_row)
    return jnp.where(allowed, 0.0, masked_score)


def attend_forward_kernel(
    heads, width, keys, info_ref, q_ref, kv_ref, start_ref, o_ref, total_ref
):
    at = pl.program_id(1)
    rows = q_ref.shape[0]
    q = stack_heads(q_ref[...], heads, width)
    start_row = start_ref[...]
    query_row = info_ref[2, at] + lax.broadcasted_iota(jnp.int32, (1, rows), 1)
    scale = width**-0.5 * log2_e

    def step(block, carried):
        top, total, mixed = carried
        first_key = pl.multiple_of(block * keys, keys)
        k = kv_ref[pl.ds(first_key, keys), :width]
        v = kv_ref[pl.ds(first_key, keys), width:]
        bias = block_bias(first_key, keys, start_row, query_row)
        scores = dot_nt(k, q) * scale + jnp.concatenate([bias] * heads, axis=1)
        new_top = jnp.maximum(top, jnp.max(scores, axis=0, keepdims=True))
        shrink = jnp.exp2(top - new_top)
        part = jnp.exp2(scores - new_top)
        total = total * shrink + jnp.sum(part, axis=0, keepdims=True)
        mixed = mixed * shrink + dot_tn(v, part.astype(bf16))
        return new_top, total, mixed

    count = heads * rows
    top, total, mixed = lax.fori_loop(
        info_ref[0, at],
        info_ref[1, at],
        step,
        (
            jnp.full((1, count), masked_score, f32),
            jnp.zeros((1, count), f32),
            jnp.zeros((width, count), f32),
        ),
    )
    out = (mixed / total).T.astype(bf16)
    for h in range(heads):
        o_ref[:, h * width : (h + 1) * width] = out[h * rows : (h + 1) * rows]
    total_ref[...] = (top + jnp.log2(total)).reshape(total_ref.shape)


def attend_backward_kernel(
    heads,
    width,
    keys,
    info_ref,
    q_ref,
    grad_ref,
    o_ref,
    kv_ref,
    start_ref,
    total_ref,
    dq_ref,
    dkv_ref,
):
    at = pl.program_id(1)
    rows = q_ref.shape[0]

    @pl.when((pl.program_id(0) == 0) & (at == 0))
    def _():
        dkv_ref[...] = jnp.zeros_like(dkv_ref)

    q = stack_heads(q_ref[...], heads, width)
    grad = stack_heads(grad_ref[...], heads, width)
    out = stack_heads(o_ref[...], heads, width)
    delta = jnp.sum((grad.astype(f32) * out.astype(f32)).T, axis=0, keepdims=True)
    count = heads * rows
    total = total_ref[...].reshape(1, count)
    start_row = start_ref[...]
    query_row = info_ref[2, at] + lax.broadcasted_iota(jnp.int32, (1, rows), 1)
    scale = width**-0.5

    def step(block, dq):
        first_key = pl.multiple_of(block * keys, keys)
        k = kv_ref[pl.ds(first_key, keys), :width]
        v = kv_ref[pl.ds(first_key, keys), width:]
        bias = block_bias(first_key, keys, start_row, query_row)
        scores = dot_nt(k, q) * (scale * log2_e) + jnp.concatenate([bias] * heads, axis=1)
        probs = jnp.exp2(scores - total)
        dprobs = dot_nt(v, grad)
        dscores = (probs * (dprobs - delta)).astype(bf16)
        dkv_ref[pl.ds(first_key, keys), :width] += dot_nn(dscores, q) * scale
        dkv_ref[pl.ds(first_key, keys), width:] += dot_nn(probs.astype(bf16), grad)
        return dq + dot_tn(k, dscores)

    dq = lax.fori_loop(
        info_ref[0, at], info_ref[1, at], step, jnp.zeros((width, count), f32)
    )
    dq = (dq * scale).T.astype(bf16)
    for h in range(heads):
        dq_ref[:, h * width : (h + 1) * width] = dq[h * rows : (h + 1) * rows]


def attend_shapes(queries, width):
    tokens = queries.shape[0]
    heads_all = queries.shape[1] // width
    heads = 16 if heads_all % 16 == 0 else heads_all
    rows = min(128, tokens)
    return tokens, heads_all, heads, heads_all // heads, rows, tokens // rows


def attend_forward(queries, kv_all, info, starts, width, keys):
    tokens, heads_all, heads, groups, rows, blocks = attend_shapes(queries, width)
    return pl.pallas_call(
        functools.partial(attend_forward_kernel, heads, width, keys),
        grid_spec=pltpu.PrefetchScalarGridSpec(
            num_scalar_prefetch=1,
            grid=(groups, blocks),
            in_specs=[
                pl.BlockSpec((rows, heads * width), lambda g, i, info: (i, g)),
                pl.BlockSpec(kv_all.shape, lambda g, i, info: (0, 0)),
                pl.BlockSpec((1, rows), lambda g, i, info: (0, i)),
            ],
            out_specs=[
                pl.BlockSpec((rows, heads * width), lambda g, i, info: (i, g)),
                pl.BlockSpec((1, 1, 1, heads * rows), lambda g, i, info: (g, i, 0, 0)),
            ],
        ),
        out_shape=[
            jax.ShapeDtypeStruct((tokens, heads_all * width), bf16),
            jax.ShapeDtypeStruct((groups, blocks, 1, heads * rows), f32),
        ],
        name="attend_forward",
    )(info, queries, kv_all, starts)


def attend_backward(queries, grad, mixed, kv_all, info, starts, totals, width, keys):
    tokens, heads_all, heads, groups, rows, blocks = attend_shapes(queries, width)
    tile = pl.BlockSpec((rows, heads * width), lambda g, i, info: (i, g))
    return pl.pallas_call(
        functools.partial(attend_backward_kernel, heads, width, keys),
        grid_spec=pltpu.PrefetchScalarGridSpec(
            num_scalar_prefetch=1,
            grid=(groups, blocks),
            in_specs=[
                tile,
                tile,
                tile,
                pl.BlockSpec(kv_all.shape, lambda g, i, info: (0, 0)),
                pl.BlockSpec((1, rows), lambda g, i, info: (0, i)),
                pl.BlockSpec((1, 1, 1, heads * rows), lambda g, i, info: (g, i, 0, 0)),
            ],
            out_specs=[
                tile,
                pl.BlockSpec(kv_all.shape, lambda g, i, info: (0, 0)),
            ],
        ),
        out_shape=[
            jax.ShapeDtypeStruct((tokens, heads_all * width), bf16),
            jax.ShapeDtypeStruct(kv_all.shape, f32),
        ],
        name="attend_backward",
    )(info, queries, grad, mixed, kv_all, starts, totals)


def after(value, *earlier):
    return lax.optimization_barrier((value, earlier))[0]


def axis_gather(block, axis):
    copies = jnp.broadcast_to(block[None], (lax.axis_size(axis),) + block.shape)
    return lax.all_to_all(copies, axis, 0, 0)


def tensor_exchange(parts, rows):
    parts = parts.reshape(lax.axis_size("tensor"), rows, parts.shape[1])
    return lax.all_to_all(parts, "tensor", 0, 0)


def tensor_swaps(parts):
    size = lax.axis_size("tensor")
    index = lax.axis_index("tensor")
    found = jnp.zeros(parts.shape, parts.dtype)
    zeros = (0,) * (parts.ndim - 1)
    for s in range(size):
        part = lax.dynamic_index_in_dim(parts, (index + s) % size, 0)
        if s:
            part = lax.ppermute(part, "tensor", [(i, (i + s) % size) for i in range(size)])
        found = lax.dynamic_update_slice(found, part, ((index - s) % size,) + zeros)
    return found


class Ring:
    def __init__(self, size):
        self.size = size
        self.chips = size // 2
        half = self.chips // 2
        if half:
            self.order = list(range(half)) + list(range(self.chips - 1, half - 1, -1))
        else:
            self.order = [0]
        n = self.chips
        self.pairs = []
        for i in range(n):
            here, there = self.order[i], self.order[(i + 1) % n]
            self.pairs += [(2 * here, 2 * there), (2 * there + 1, 2 * here + 1)]
        self.swap_pairs = [(i, i ^ 1) for i in range(size)]
        self.keys = [(s, c) for s in range(n) for c in (0, 1)]

    def owner(self, index, s, c):
        place = [0] * self.chips
        for i, chip in enumerate(self.order):
            place[chip] = i
        at = jnp.array(place, jnp.int32)[index // 2]
        core = index % 2 if c == 0 else 1 - index % 2
        at = (at + jnp.where(core == 0, -s, s)) % self.chips
        return 2 * jnp.array(self.order, jnp.int32)[at] + core

    def step(self, value):
        return lax.ppermute(value, "dp", self.pairs)

    def swap(self, value):
        return lax.ppermute(value, "dp", self.swap_pairs)

    def gather(self, own, gates=()):
        blocks = {(0, 0): own, (0, 1): self.swap(own)}
        for s in range(1, self.chips):
            if s < len(gates) and gates[s] is not None:
                own = after(own, gates[s])
            own = self.step(own)
            blocks[(s, 0)] = own
            blocks[(s, 1)] = self.swap(own)
        return blocks

    def sums(self, parts):
        held = None
        gate = yield
        for s in list(range(1, self.chips)) + [0]:
            there = self.swap(parts[(s, 1)].astype(bf16))
            if gate is not None:
                there = after(there, gate)
            shares = [parts[(s, 0)], there] + ([] if held is None else [held])
            if s:
                value = total(shares).astype(bf16)
                held = self.step(value)
                gate = yield value
            else:
                gate = yield shares


def total(shares):
    return sum(share.astype(f32) for share in shares)


def started(sums):
    next(sums)
    return sums


def units_kernel(count, piece, tiles, *refs):
    seconds, grads = refs[:count], refs[count : 2 * count]
    rows_ref, cols_ref, shift_ref = refs[2 * count : 2 * count + 3]
    outs = refs[2 * count + 3 :]
    actives, pres, shares, lasts = (outs[k * count : (k + 1) * count] for k in range(4))
    active_kept, pre_kept = (outs[k * count : (k + 1) * count] for k in (4, 5))
    at = pl.program_id(0)

    def pieces(block, first):
        width = block.shape[1]
        return jnp.concatenate(
            [block[:, k : k + piece] for k in range(first * piece, width, 2 * piece)], axis=1
        )

    @pl.when(at < tiles)
    def _():
        up, down = pieces(rows_ref, 0), pieces(rows_ref, 1)
        for k in range(count):
            preact = dot_nt(seconds[k][...], up) + shift_ref[...]
            grad_active = dot_nt(grads[k][...], down)
            value, slope = gelu_both(preact)
            value = value.astype(bf16)
            pre = (grad_active * slope).astype(bf16)
            actives[k][...] = value
            pres[k][...] = pre
            active_kept[k][at] = value
            pre_kept[k][at] = pre

    @pl.when(at >= tiles)
    def _():
        up, down = pieces(cols_ref, 0), pieces(cols_ref, 1)
        for k in range(count):
            pre = jnp.concatenate([pre_kept[k][j] for j in range(tiles)], axis=1)
            shares[k][...] = dot_nn(pre, up).astype(bf16)
            value = jnp.concatenate([active_kept[k][j] for j in range(tiles)], axis=1)
            lasts[k][...] = dot_nn(value, down).astype(bf16)


def units(seconds, grads, weights, piece, shift):
    count = len(seconds)
    rows, model = seconds[0].shape
    hidden = weights.shape[0]
    width = min(256, hidden)
    tiles = hidden // width
    turns = model // (2 * piece)
    tile = pl.BlockSpec((rows, width), lambda j: (0, jnp.minimum(j, tiles - 1)))
    whole = pl.BlockSpec((rows, model), lambda j: (0, 0))
    part = pl.BlockSpec((rows, 2 * piece), lambda j: (0, jnp.maximum(j - tiles, 0)))
    out = pl.pallas_call(
        functools.partial(units_kernel, count, piece, tiles),
        grid=(tiles + turns,),
        in_specs=[whole] * (2 * count)
        + [
            pl.BlockSpec((width, 2 * model), lambda j: (jnp.minimum(j, tiles - 1), 0)),
            pl.BlockSpec((hidden, 4 * piece), lambda j: (0, jnp.maximum(j - tiles, 0))),
            pl.BlockSpec((1, width), lambda j: (0, jnp.minimum(j, tiles - 1))),
        ],
        out_specs=[tile] * (2 * count) + [part] * (2 * count),
        out_shape=[jax.ShapeDtypeStruct((rows, hidden), bf16)] * (2 * count)
        + [jax.ShapeDtypeStruct((rows, model), bf16)] * (2 * count),
        scratch_shapes=[pltpu.VMEM((tiles, rows, width), bf16)] * (2 * count),
        cost_estimate=pl.CostEstimate(
            flops=8 * count * rows * model * hidden,
            transcendentals=count * rows * hidden,
            bytes_accessed=8 * hidden * model + 4 * count * rows * (2 * model + hidden),
        ),
        name="units",
    )(*seconds, *grads, weights, weights, shift.reshape(1, hidden))
    return [out[k * count : (k + 1) * count] for k in range(4)]


def rows_product_kernel(depth, owner_ref, left_ref, shift_ref, *refs):
    blocks, out_ref = refs[:-1], refs[-1]
    total = jnp.broadcast_to(shift_ref[...], out_ref.shape)
    for k, block in enumerate(blocks):
        at = pl.multiple_of(owner_ref[k] * depth, depth)
        total = total + dot_nn(left_ref[:, pl.ds(at, depth)], block[...])
    out_ref[...] = total.astype(out_ref.dtype)


def rows_product(left, blocks, owners, shift):
    depth, width = blocks[0].shape
    tile = 128 * max(t for t in range(1, 9) if width % (128 * t) == 0)
    return pl.pallas_call(
        functools.partial(rows_product_kernel, depth),
        grid_spec=pltpu.PrefetchScalarGridSpec(
            num_scalar_prefetch=1,
            grid=(width // tile,),
            in_specs=[
                pl.BlockSpec(left.shape, lambda j, owner: (0, 0)),
                pl.BlockSpec((1, tile), lambda j, owner: (0, j)),
            ]
            + [pl.BlockSpec((depth, tile), lambda j, owner: (0, j)) for _ in blocks],
            out_specs=pl.BlockSpec((left.shape[0], tile), lambda j, owner: (0, j)),
        ),
        out_shape=jax.ShapeDtypeStruct((left.shape[0], width), bf16),
        cost_estimate=pl.CostEstimate(
            flops=2 * left.shape[0] * left.shape[1] * width,
            transcendentals=0,
            bytes_accessed=2 * left.shape[1] * width,
        ),
        name="rows_product",
    )(owners, left, shift.reshape(1, width), *blocks)


def grads_product_kernel(count, *refs):
    out_ref, sum_ref = refs[2 * count :]
    total = dot_tn(refs[0][...], refs[count][...])
    for k in range(1, count):
        total = total + dot_tn(refs[k][...], refs[count + k][...])
    out_ref[...] = total.astype(out_ref.dtype)

    @pl.when(pl.program_id(0) == 0)
    def _():
        sums = jnp.zeros(sum_ref.shape, f32)
        for k in range(count):
            sums = sums + jnp.sum(refs[k][...].astype(f32), axis=0, keepdims=True)
        sum_ref[...] = sums


def grads_product(lefts, rights):
    rows, units = lefts[0].shape
    width = rights[0].shape[1]
    tile = min(512, width)
    count = len(lefts)
    return pl.pallas_call(
        functools.partial(grads_product_kernel, count),
        grid=(width // tile,),
        in_specs=[pl.BlockSpec((rows, units), lambda j: (0, 0)) for _ in lefts]
        + [pl.BlockSpec((rows, tile), lambda j: (0, j)) for _ in rights],
        out_specs=[
            pl.BlockSpec((units, tile), lambda j: (0, j)),
            pl.BlockSpec((1, units), lambda j: (0, 0)),
        ],
        out_shape=[
            jax.ShapeDtypeStruct((units, width), bf16),
            jax.ShapeDtypeStruct((1, units), f32),
        ],
        cost_estimate=pl.CostEstimate(
            flops=2 * count * rows * units * width,
            transcendentals=0,
            bytes_accessed=2 * count * rows * (units + width) + 2 * units * width,
        ),
        name="grads_product",
    )(*lefts, *rights)


def cols_product_kernel(depth, owner_ref, left_ref, *refs):
    blocks, out_ref = refs[:-1], refs[-1]
    left = left_ref[...]
    for k, block in enumerate(blocks):
        at = pl.multiple_of(owner_ref[k] * depth, depth)
        out_ref[:, pl.ds(at, depth)] = dot_nt(left, block[...])


def cols_product(left, blocks, owners):
    depth, width = blocks[0].shape
    rows = left.shape[0]
    out_width = depth * len(blocks)
    return pl.pallas_call(
        functools.partial(cols_product_kernel, depth),
        grid_spec=pltpu.PrefetchScalarGridSpec(
            num_scalar_prefetch=1,
            grid=(left.shape[0] // rows,),
            in_specs=[pl.BlockSpec((rows, width), lambda i, owner: (i, 0))]
            + [pl.BlockSpec((depth, width), lambda i, owner: (0, 0)) for _ in blocks],
            out_specs=pl.BlockSpec((rows, out_width), lambda i, owner: (i, 0)),
        ),
        out_shape=jax.ShapeDtypeStruct((left.shape[0], out_width), f32),
        cost_estimate=pl.CostEstimate(
            flops=2 * left.shape[0] * out_width * width,
            transcendentals=0,
            bytes_accessed=2 * out_width * width,
        ),
        name="cols_product",
    )(owners, left, *blocks)


def on_device(
    tokens,
    segment_ids,
    attngain,
    attnshift,
    queryweight,
    querybias,
    keyvalue,
    valuebias,
    outweight,
    outbias,
    mlpgain,
    mlpshift,
    upweight,
    upbias,
    downweight,
    downbias,
    cotangent,
):
    head_dim = valuebias.shape[0]
    count, model = tokens.shape
    n_dp = lax.axis_size("dp")
    n_tensor = lax.axis_size("tensor")
    dp_index = lax.axis_index("dp")
    tensor_index = lax.axis_index("tensor")
    ring = Ring(n_dp)
    order = ring.keys
    owners = jnp.stack([ring.owner(dp_index, *key) for key in order]).astype(jnp.int32)
    segment = segment_ids[0]
    length = segment.shape[0]
    rows = tokens.astype(f32)
    depth = queryweight.shape[0]
    width = queryweight.shape[1]

    both = lax.all_gather(jnp.stack([queryweight, outweight.T]), "tensor", axis=0)
    both = both.transpose(1, 2, 0, 3).reshape(2, depth, n_tensor * width)

    hidden_own = upweight.shape[1] // n_dp
    bias_part = lax.dynamic_slice_in_dim(upbias, dp_index * hidden_own, hidden_own)
    biases = axis_gather(jnp.concatenate([querybias, bias_part]), "tensor")
    query_shift = biases[:, :width].reshape(-1)
    up_shift = biases[:, width:].reshape(-1)
    pair_full = axis_gather(after(keyvalue, biases), "dp").reshape(model, 2 * head_dim)

    first_mean, first_scale = norm_stats(rows)
    normed_first = ((rows - first_mean) * first_scale * attngain + attnshift).astype(bf16)
    pair_shift = jnp.concatenate([jnp.zeros((head_dim,), f32), valuebias])
    pairs = (dot_nn(normed_first, pair_full) + pair_shift).astype(bf16)

    weights = after(jnp.concatenate([upweight.T, downweight], axis=1), pair_full)
    weights = lax.all_to_all(weights, "dp", 0, 1, tiled=True)
    kv_all = axis_gather(after(pairs, weights), "tensor").reshape(length, 2 * head_dim)

    first_blocks = ring.gather(both[0], (None, None, weights, kv_all))
    first_list = [first_blocks[key] for key in order]
    weights = lax.all_gather(after(weights, kv_all), "tensor", axis=0, tiled=True)

    grads = {(0, 0): cotangent, (1, 0): ring.step(cotangent)}
    normed_late = after(normed_first, grads[(1, 0)])
    queries = rows_product(normed_late, first_list, owners, query_shift)
    if ring.chips > 2:
        grads[(2, 0)] = ring.step(after(grads[(1, 0)], queries))
    keys = 256 if length % 256 == 0 else 128
    query_block = min(128, count)
    first_row = tensor_index * count
    own_segment = lax.dynamic_slice_in_dim(segment, first_row, count)
    starts = jnp.sum(
        (segment[None, :] < own_segment[:, None]).astype(jnp.int32), axis=1
    )
    block_first = first_row + jnp.arange(count // query_block, dtype=jnp.int32) * query_block
    info = jnp.stack(
        [
            starts[::query_block] // keys,
            (block_first + query_block - 1) // keys + 1,
            block_first,
        ]
    ).astype(jnp.int32)
    starts = starts.reshape(1, count)
    mixed, totals = attend_forward(queries, kv_all, info, starts, head_dim, keys)
    for at in range(3, ring.chips):
        grads[(at, 0)] = ring.step(after(grads[(at - 1, 0)], mixed))
    for at in range(ring.chips):
        grads[(at, 1)] = ring.swap(after(grads[(at, 0)], mixed))
    out_blocks = ring.gather(both[1], (None, first_list, queries, mixed))
    out_list = [out_blocks[key] for key in order]
    residual = rows + cols_product(after(mixed, grads[(min(2, ring.chips - 1), 0)]), out_list, owners) + outbias
    second_mean, second_scale = norm_stats(residual)
    normed_second = ((residual - second_mean) * second_scale * mlpgain + mlpshift).astype(bf16)

    active, grad_pre, second_parts, last_parts, seconds = {}, {}, {}, {}, {}
    done = []

    def work(s):
        keys_here = [(s, 0), (s, 1)]
        seconds[keys_here[0]] = passed[s]
        seconds[keys_here[1]] = ring.swap(after(passed[s], done))
        found = units(
            [after(seconds[key], done[-1:]) for key in keys_here],
            [grads[key] for key in keys_here],
            weights,
            depth,
            up_shift,
        )
        done.append(found[2])
        for kept, values in zip((active, grad_pre, second_parts, last_parts), found):
            kept.update(zip(keys_here, values))

    passed = [normed_second]
    for s in range(1, ring.chips):
        if s >= 3:
            work(s - 2)
        passed.append(ring.step(after(passed[-1], done)))
    for s in range(max(1, ring.chips - 2), ring.chips):
        work(s)
    work(0)
    sums = started(ring.sums(second_parts))
    for at in range(ring.chips):
        grad_second = sums.send(done[min(at + 1, len(done) - 1)])
    parts_done = done[-1]
    up_local, upbias_part = grads_product(
        [after(grad_pre[key], parts_done) for key in order], [seconds[key] for key in order]
    )
    up_part = lax.psum_scatter(up_local, "tensor", scatter_dimension=0, tiled=True)
    grad_second = [after(share, up_local) for share in grad_second]
    grad_second += [jnp.zeros_like(cotangent)] * (3 - len(grad_second))

    grad_resid, grad_branch, second_sums = norm_backward_shares(
        grad_second, residual, cotangent, mlpgain
    )
    grad_mixed = rows_product(grad_branch, out_list, owners, jnp.zeros((model,), f32))
    grad_queries, grad_kv = attend_backward(
        queries, grad_mixed, mixed, kv_all, info, starts, totals, head_dim, keys
    )

    def depth_sums(local):
        return started(
            ring.sums(
                {
                    key: lax.dynamic_slice_in_dim(local, owners[k] * depth, depth, 0)
                    for k, key in enumerate(order)
                }
            )
        )

    def width_owner(block):
        parts = block.astype(bf16).reshape(depth, n_tensor, width).transpose(1, 0, 2)
        return lax.psum_scatter(parts, "tensor", scatter_dimension=0, tiled=False).astype(f32)

    chips = ring.chips
    last_sums = started(ring.sums(last_parts))
    last_sent = [last_sums.send(gate) for gate in (grad_mixed, grad_queries)[:chips]]
    pair_raw = tensor_exchange(grad_kv.astype(bf16), count)
    down_local, _ = grads_product(
        [after(active[key], grad_queries, last_sent) for key in order],
        [grads[key] for key in order],
    )
    down_part = lax.psum_scatter(down_local, "tensor", scatter_dimension=0, tiled=True)
    out_local = dot_tn(after(grad_branch, down_local), mixed).astype(bf16)
    out_sums = depth_sums(out_local)
    out_sent = [out_sums.send(None)]
    if chips > 2:
        last_sent.append(last_sums.send(down_local))
    pair_shares = after(pair_raw, down_local)
    grad_pairs = jnp.sum(pair_shares.astype(f32), axis=0).astype(bf16)
    grad_qkv = jnp.concatenate([grad_queries, grad_pairs], axis=1)
    first_local = dot_tn(normed_first, grad_qkv).astype(bf16)
    first_sums = depth_sums(first_local)
    first_sent = [first_sums.send(None) for _ in range(chips)]
    first_part = total(first_sent[-1])
    for at in range(1, chips):
        out_sent.append(out_sums.send(first_part))
    out_part = total(out_sent[-1])
    for at in range(len(last_sent), chips):
        last_sent.append(last_sums.send(first_part))
    layer_out = residual + total(last_sent[-1]) + downbias
    up_grad = lax.all_to_all(after(up_part, first_sent[-2]), "dp", 1, 0, tiled=True).astype(f32).T
    grad_first = cols_product(after(grad_queries, first_sent[min(1, chips - 1)]), first_list, owners)
    grad_first = grad_first + dot_nt(grad_pairs, pair_full)
    grad_one, attngain_part, attnshift_part = norm_backward(
        rows, first_mean, first_scale, attngain, grad_first
    )
    tokens_grad = (grad_resid + grad_one).astype(bf16)

    shift_part = jnp.sum(grad_qkv.astype(f32), axis=0)
    vectors = [
        attngain_part,
        attnshift_part,
        second_sums[0],
        second_sums[1],
        second_sums[2],
        second_sums[3],
        shift_part[:model],
        shift_part[model + head_dim :],
    ]
    sizes = [v.shape[0] for v in vectors]
    plain = sum(sizes)
    flat = jnp.concatenate(vectors + [upbias_part[0]])
    flat = axis_gather(flat, "dp")
    units_flat = flat[:, plain:].reshape(n_dp, n_tensor, hidden_own)
    units_flat = units_flat.transpose(1, 0, 2).reshape(n_tensor, n_dp * hidden_own)
    flat = jnp.broadcast_to(jnp.sum(flat[:, :plain], axis=0), (n_tensor, plain))
    flat = jnp.concatenate([flat, units_flat], axis=1)

    first_sent = first_part.astype(bf16)
    first_sent = jnp.concatenate(
        [
            first_sent[:, :model].reshape(depth, n_tensor, width).transpose(1, 0, 2),
            jnp.broadcast_to(first_sent[None, :, model:], (n_tensor, depth, 2 * head_dim)),
        ],
        axis=2,
    )
    first_sent = tensor_swaps(first_sent)
    down_grad = lax.all_to_all(after(down_part, up_grad), "dp", 1, 0, tiled=True).astype(f32)
    out_grad = width_owner(after(out_part, first_sent)).T
    flat = lax.all_to_all(after(flat, down_grad), "tensor", 0, 0, tiled=True)
    flat = jnp.sum(flat, axis=0)
    first_grad = jnp.sum(first_sent.astype(f32), axis=0)
    query_grad = first_grad[:, :width]
    keyvalue_grad = first_grad[:, width:]

    upbias_grad = flat[plain : plain + n_dp * hidden_own]
    found = []
    at = 0
    for size in sizes:
        found.append(flat[at : at + size])
        at += size
    attngain_grad, attnshift_grad, mlpgain_grad, mlpshift_grad = found[:4]
    outbias_grad, downbias_grad, query_shift_grad, valuebias_grad = found[4:]
    querybias_grad = lax.dynamic_slice_in_dim(query_shift_grad, tensor_index * width, width)
    return (
        layer_out.astype(bf16),
        tokens_grad,
        attngain_grad,
        attnshift_grad,
        query_grad,
        querybias_grad,
        keyvalue_grad,
        valuebias_grad,
        out_grad,
        outbias_grad,
        mlpgain_grad,
        mlpshift_grad,
        up_grad,
        upbias_grad,
        down_grad,
        downbias_grad,
    )


def solution(mesh):
    return jax.shard_map(
        on_device,
        mesh=mesh,
        in_specs=(
            P(("dp", "tensor"), None),
            P("dp", None),
            P(),
            P(),
            P("dp", "tensor"),
            P("tensor"),
            P("dp", None),
            P(),
            P("tensor", "dp"),
            P(),
            P(),
            P(),
            P("dp", "tensor"),
            P("tensor"),
            P("tensor", "dp"),
            P(),
            P(("dp", "tensor"), None),
        ),
        out_specs=(
            P(("dp", "tensor"), None),
            P(("dp", "tensor"), None),
            P(),
            P(),
            P("dp", "tensor"),
            P("tensor"),
            P("dp", None),
            P(),
            P("tensor", "dp"),
            P(),
            P(),
            P(),
            P("dp", "tensor"),
            P("tensor"),
            P("tensor", "dp"),
            P(),
        ),
        check_vma=False,
    )
```
